512 devices in a mesh: tgt: 128 (over x, z, core), band: 4 (over y).
Axes of the slice: x: 4, y: 4, z: 16, core: 2. Of those that a mesh axis runs over, the one named last changes fastest.
Arguments:
- exposure_flux: bfloat16 [16384, 4096], P('tgt', 'band'), may hold values from -6 to 6
- exposure_ivar: bfloat16 [16384, 4096], P('tgt', 'band'), may hold values from 0.19921875 to 5
- exposure_res: bfloat16 [16384, 11, 4096], P('tgt', None, 'band'), may hold values from 0 to 1
- target_of_row: int32 [16384], replicated, may hold values from 0 to 2047, as said below
- valid_of_row: int32 [16384], replicated, may hold values from 0 to 1, as said below
- rest_basis: float32 [10, 4608], replicated, may hold values from -6 to 6
- redshift_shift: int32 [32], replicated, may hold values from 0 to 511
Outputs:
- coadd_flux: float32 [2048, 4096], P('tgt', 'band')
- coadd_res: bfloat16 [2048, 11, 4096], P('tgt', None, 'band')
- fit_gain: float32 [2048, 32], P('tgt', 'band')
The draws below stay inside these ranges and needn't reach their ends.
Inputs may be any that keep to these rules, and one draw needn't show every extreme that they name: `target_of_row`: every target has exactly 8 rows. The rows held by one index of tgt (rows j * 128 to (j + 1) * 128 - 1) include at most 2 rows of the targets of any one owner, where the owner of target t is t // 16; some pairs reach 2. `valid_of_row`: every target has at least one row with flag 1.
All inputs are finite; a program needn't handle non-finite values.
Results may differ from the reference program's by a relative error of at most 0.004.
Values may be sent and summed in bfloat16 or wider, within the bound.
No kernel may reach another device: no remote copies, remote signals or barrier semaphores. Data moves between devices by JAX's collectives and lax.ppermute only.
A program may use at most 128 MiB of HBM per device.

```python
import math
import jax
import jax.numpy as jnp
import numpy as np
from jax import lax

TGT_DEV = 16
SLOTS = 8
NDIAG = 11
NB = 10
SHIFT = 512
OWNERS = 128
TARGETS = 2048
EXP_DEV = 128
EXPOSURES = 16384
CAP = 2
NW = 4096
NZ = 32
NREST = 4608


def routing(key):
    owners = OWNERS
    row_count = EXP_DEV
    capacity = CAP
    key_order, key_slots, key_rows, key_first, key_coin = jax.random.split(key, 5)
    rank_of = jnp.argsort(jax.random.permutation(key_order, owners)).astype(jnp.int32)
    values = jnp.arange(owners, dtype=jnp.int32)
    score = jnp.where(values == owners - 1, -3, jnp.where(values == 1, -2, jnp.where(values == owners // 2, -1, rank_of)))
    offset_order = jnp.argsort(score, stable=True).astype(jnp.int32)
    slot_ids = jnp.arange(row_count, dtype=jnp.int32)
    half_rows = row_count // 2
    groups = jnp.where(slot_ids < half_rows, slot_ids // capacity, owners // 4 + (slot_ids - half_rows) // (capacity // 2))
    offsets = offset_order[groups]

    def one_receiver(slot_key):
        return jax.random.permutation(slot_key, row_count)
    slot_order = jax.vmap(one_receiver)(jax.random.split(key_slots, owners))
    slot_offset = offsets[slot_order]
    receiver = jnp.arange(owners, dtype=jnp.int32)[:, None]
    source = (receiver + slot_offset) % owners
    rank_order = jax.random.permutation(key_rows, owners * row_count).astype(jnp.int32)
    sort_keys = source.reshape(-1).astype(jnp.int32) * (owners * row_count) + rank_order
    row_order = jnp.argsort(sort_keys)
    flat_ids = jnp.arange(owners * row_count, dtype=jnp.int32)
    receiver_flat = flat_ids // row_count
    slot_flat = flat_ids % row_count
    target = receiver_flat * TGT_DEV + slot_flat // SLOTS
    first_valid = jax.random.randint(key_first, (owners * TGT_DEV,), 0, SLOTS)
    coin_flip = jax.random.randint(key_coin, (owners * row_count,), 0, 10)
    valid_flag = jnp.logical_or(slot_flat % SLOTS == first_valid[target], coin_flip < 6)
    return (target[row_order].astype(jnp.int32), valid_flag[row_order].astype(jnp.int32))


def draw_target_of_row(key, part):
    return routing(key)[0]


def draw_valid_of_row(key, part):
    return routing(key)[1]


def place_ends(values, own_key, smallest, largest):
    dims = values.shape
    spot = [jax.random.randint(jax.random.fold_in(own_key, axis), (), 0, dims[axis]) for axis in range(len(dims))]
    values = values.at[tuple(spot)].set(smallest)
    longest = dims.index(max(dims))
    spot[longest] = (spot[longest] + 1) % dims[longest]
    return values.at[tuple(spot)].set(largest)


def levels(stream_key, dims, shards, least, largest):
    level, own = 1.0, jax.random.fold_in(stream_key, 6)
    for position, shards_of in shards:
        draws = jnp.exp(jax.random.uniform(jax.random.fold_in(own, position), (shards_of,), jnp.float32, least / len(shards), largest / len(shards)))
        level = level * jnp.repeat(draws, dims[position] // shards_of).reshape([-1 if axis == position else 1 for axis in range(len(dims))])
    return level


def noise(rng, shape, spread, limit, cuts=(), kind=jnp.bfloat16):
    level = levels(rng, shape, cuts, -0.22, 0.18) if cuts else 1.0
    result = jax.random.normal(rng, shape, jnp.float32) * spread * level
    return jnp.minimum(jnp.maximum(result, -limit), limit).astype(kind)


def setup_inputs(seed: int = 0) -> dict:
    seeds = jax.random.split(jax.random.key(seed), 8)
    return {
        "exposure_flux": noise(seeds[0], (EXPOSURES, NW), 1.0, 6.0, ((0, 128), (1, 4))),
        "exposure_ivar": jnp.clip(jnp.exp(math.log(5.0) - 3.2227897 * jax.random.uniform(seeds[1], (EXPOSURES, NW), jnp.float32) ** levels(seeds[1], (EXPOSURES, NW), ((0, 128), (1, 4)), -0.2, 0.2)), 0.19921875, 5.0).astype(jnp.bfloat16),
        "exposure_res": jnp.clip(1.0 * jax.random.uniform(seeds[2], (EXPOSURES, NDIAG, NW), jnp.float32) ** levels(seeds[2], (EXPOSURES, NDIAG, NW), ((0, 128), (2, 4)), -0.2, 0.2), 0.0, 1.0).astype(jnp.bfloat16),
        "target_of_row": draw_target_of_row(jax.random.fold_in(seeds[7], 71), 0),
        "valid_of_row": draw_valid_of_row(jax.random.fold_in(seeds[7], 71), 0),
        "rest_basis": noise(seeds[5], (NB, NREST), 1.0, 6.0, (), jnp.float32),
        "redshift_shift": place_ends(jax.random.randint(seeds[6], (NZ,), 0, SHIFT), jax.random.fold_in(seeds[6], 1), 0, SHIFT - 1).astype(jnp.int32),
    }


pair_first, pair_second = np.triu_indices(10)


def solve_normal(matrix, right_side):
    basis_count = right_side.shape[0]
    rows_of = [[None] * basis_count for column in range(basis_count)]
    for p in range(len(pair_first)):
        b = int(pair_first[p])
        c = int(pair_second[p])
        rows_of[b][c] = matrix[p]
        rows_of[c][b] = matrix[p]
    vector = [right_side[b] for b in range(basis_count)]
    for k in range(basis_count):
        inverse = 1.0 / rows_of[k][k]
        for r in range(k + 1, basis_count):
            factor = rows_of[r][k] * inverse
            for c in range(k + 1, basis_count):
                rows_of[r][c] = rows_of[r][c] - factor * rows_of[k][c]
            vector[r] = vector[r] - factor * vector[k]
    answer = [None] * basis_count
    for k in reversed(range(basis_count)):
        running = vector[k]
        for c in range(k + 1, basis_count):
            running = running - rows_of[k][c] * answer[c]
        answer[k] = running / rows_of[k][k]
    gain_total = right_side[0] * answer[0]
    for b in range(1, basis_count):
        gain_total = gain_total + right_side[b] * answer[b]
    return gain_total


def basis_windows(rest_basis, shifts, first_wave, length):
    def one_shift(shift_value):
        return lax.dynamic_slice_in_dim(rest_basis, (first_wave + shift_value).astype(jnp.int32), length, axis=1)
    return jax.vmap(one_shift)(shifts)


def normal_terms(weight_sum, flux_sum, windows):
    products = windows[:, pair_first, :] * windows[:, pair_second, :]
    matrix = jnp.einsum('ti,zpi->ztp', weight_sum, products, precision=lax.Precision.HIGHEST)
    right_side = jnp.einsum('ti,zbi->ztb', flux_sum, windows, precision=lax.Precision.HIGHEST)
    return matrix, right_side


def blocked_normals(weight_sum, flux_sum, rest_basis, shifts, first_wave, length):
    total_shifts = shifts.shape[0]
    block_size = 8 if total_shifts % 8 == 0 else total_shifts
    grouped = shifts.reshape(total_shifts // block_size, block_size)

    def one_block(shift_block):
        return normal_terms(weight_sum, flux_sum, basis_windows(rest_basis, shift_block, first_wave, length))

    matrix, right_side = lax.map(one_block, grouped)
    return (matrix.reshape((total_shifts,) + matrix.shape[2:]),
            right_side.reshape((total_shifts,) + right_side.shape[2:]))


def fit_from(matrix, right_side):
    pairs = jnp.transpose(matrix, (2, 0, 1)).reshape(matrix.shape[2], -1)
    sides = jnp.transpose(right_side, (2, 0, 1)).reshape(right_side.shape[2], -1)
    gain = solve_normal(pairs, sides).reshape(matrix.shape[0], matrix.shape[1])
    return gain.T


def reference(exposure_flux, exposure_ivar, exposure_res, target_of_row, valid_of_row, rest_basis, redshift_shift):
    weight = exposure_ivar.astype(jnp.float32) * valid_of_row.astype(jnp.float32)[:, None]
    weight_sum = jax.ops.segment_sum(weight, target_of_row, num_segments=TARGETS)
    flux_sum = jax.ops.segment_sum(weight * exposure_flux.astype(jnp.float32), target_of_row, num_segments=TARGETS)
    block_rows = EXP_DEV * 4
    block_total = EXPOSURES // block_rows
    res_blocks = exposure_res.reshape(block_total, block_rows, NDIAG, NW)
    weight_blocks = weight.reshape(block_total, block_rows, NW)
    target_blocks = target_of_row.reshape(block_total, block_rows)

    def add_block(carry, pieces):
        res_piece, weight_piece, target_piece = pieces
        update = weight_piece[:, None, :] * res_piece.astype(jnp.float32)
        return carry.at[target_piece].add(update), None

    res_sum, unused = lax.scan(add_block, jnp.zeros((TARGETS, NDIAG, NW), jnp.float32),
                               (res_blocks, weight_blocks, target_blocks))
    coadd_flux = flux_sum / weight_sum
    coadd_res = (res_sum / weight_sum[:, None, :]).astype(jnp.bfloat16)
    matrix, right_side = blocked_normals(weight_sum, flux_sum, rest_basis, redshift_shift, 0, NW)
    fit_gain = fit_from(matrix, right_side)
    return coadd_flux, coadd_res, fit_gain
```

```python
import jax
import jax.numpy as jnp
import numpy as np
from jax import lax
from jax.experimental import pallas as pl
from jax.experimental.pallas import tpu as pltpu
from jax.sharding import PartitionSpec as P

TGT_DEV = 16
NDIAG = 11
Z_DEV = 8

XS, ZS, CS = 4, 16, 2
PLANE = XS * CS
QROWS = PLANE * TGT_DEV


def place(x, z, c):
    return ((x % XS) * ZS + z % ZS) * CS + c % CS


plane_groups = [[place(x, z, c) for x in range(XS) for c in range(CS)] for z in range(ZS)]
ring_groups = [[place(x, z, c) for z in range(ZS)] for x in range(XS) for c in range(CS)]


def ring_step(values, step):
    pairs = [
        (place(x, z, c), place(x, z + step, c))
        for x in range(XS)
        for z in range(ZS)
        for c in range(CS)
    ]
    return lax.ppermute(values, "tgt", pairs)


pair_first, pair_second = np.triu_indices(10)


def solve_normal(matrix, right_side):
    basis_count = right_side.shape[0]
    rows_of = [[None] * basis_count for column in range(basis_count)]
    for p in range(len(pair_first)):
        b = int(pair_first[p])
        c = int(pair_second[p])
        rows_of[b][c] = matrix[p]
        rows_of[c][b] = matrix[p]
    vector = [right_side[b] for b in range(basis_count)]
    for k in range(basis_count):
        inverse = 1.0 / rows_of[k][k]
        for r in range(k + 1, basis_count):
            factor = rows_of[r][k] * inverse
            for c in range(k + 1, basis_count):
                rows_of[r][c] = rows_of[r][c] - factor * rows_of[k][c]
            vector[r] = vector[r] - factor * vector[k]
    answer = [None] * basis_count
    for k in reversed(range(basis_count)):
        running = vector[k]
        for c in range(k + 1, basis_count):
            running = running - rows_of[k][c] * answer[c]
        answer[k] = running / rows_of[k][k]
    gain_total = right_side[0] * answer[0]
    for b in range(1, basis_count):
        gain_total = gain_total + right_side[b] * answer[b]
    return gain_total


def basis_windows(rest_basis, shifts, first_wave, length):

    def one_shift(shift_value):
        return lax.dynamic_slice_in_dim(rest_basis, first_wave + shift_value, length, axis=1)

    return jax.vmap(one_shift)(shifts)


def normal_terms(weight_sum, flux_sum, windows):
    products = windows[:, pair_first, :] * windows[:, pair_second, :]
    matrix = jnp.einsum("ti,zpi->ztp", weight_sum, products, precision=lax.Precision.HIGHEST)
    right_side = jnp.einsum("ti,zbi->ztb", flux_sum, windows, precision=lax.Precision.HIGHEST)
    return (matrix, right_side)


def fit_from(matrix, right_side):
    pairs = jnp.transpose(matrix, (2, 0, 1)).reshape(matrix.shape[2], -1)
    sides = jnp.transpose(right_side, (2, 0, 1)).reshape(right_side.shape[2], -1)
    gain = solve_normal(pairs, sides).reshape(matrix.shape[0], matrix.shape[1])
    return gain.T


GROUP = 4


def pack_kernel(ivar_ref, flux_ref, res_ref, out_ref):
    out_ref[0, 0] = ivar_ref[...]
    out_ref[0, 1] = flux_ref[...]
    for diagonal in range(NDIAG):
        out_ref[0, 2 + diagonal] = res_ref[diagonal]


def pack(ivar, flux, res):
    row_count, wave_dev = ivar.shape
    lanes = wave_dev // PLANE
    planes = NDIAG + 2
    return pl.pallas_call(
        pack_kernel,
        out_shape=jax.ShapeDtypeStruct((PLANE, planes, row_count, lanes), ivar.dtype),
        grid=(PLANE,),
        in_specs=[
            pl.BlockSpec((row_count, lanes), lambda i: (0, i)),
            pl.BlockSpec((row_count, lanes), lambda i: (0, i)),
            pl.BlockSpec((NDIAG, row_count, lanes), lambda i: (0, 0, i)),
        ],
        out_specs=pl.BlockSpec((1, planes, row_count, lanes), lambda i: (i, 0, 0, 0)),
        cost_estimate=pl.CostEstimate(
            flops=0, bytes_accessed=4 * planes * row_count * wave_dev, transcendentals=0
        ),
    )(ivar, flux, res)


def coadd_kernel(target_ref, rows_ref, sums_ref, res_ref, terms):
    sources, planes, row_count, lanes = rows_ref.shape
    step = pl.program_id(0)

    @pl.when(step == 0)
    def fill_terms():
        def one_source(source, carry):
            rows = pl.ds(pl.multiple_of(source * row_count, row_count), row_count)
            weight = rows_ref[source, 0].astype(jnp.float32)
            terms[rows, 0:lanes] = rows_ref[source, 0]
            product = weight * rows_ref[source, 1].astype(jnp.float32)
            rounded = product.astype(jnp.bfloat16)
            terms[rows, lanes : 2 * lanes] = rounded
            rest = product - rounded.astype(jnp.float32)
            terms[rows, 2 * lanes : 3 * lanes] = rest.astype(jnp.bfloat16)
            for plane in range(2, planes):
                product = weight * rows_ref[source, plane].astype(jnp.float32)
                terms[rows, (plane + 1) * lanes : (plane + 2) * lanes] = product.astype(
                    jnp.bfloat16
                )
            return carry

        lax.fori_loop(0, sources, one_source, 0)

    per_x = CS * TGT_DEV
    local = lax.broadcasted_iota(jnp.int32, (GROUP * QROWS, 1), 0)
    q = local % QROWS
    plane_z = step * GROUP + local // QROWS
    wanted = (q // per_x) * (ZS * per_x) + plane_z * per_x + q % per_x
    member = jnp.where(target_ref[...] == wanted, 1.0, 0.0).astype(jnp.bfloat16)
    sums = jnp.dot(member, terms[...], preferred_element_type=jnp.float32)
    for g in range(GROUP):
        block = sums[g * QROWS : (g + 1) * QROWS]
        sums_ref[g, 0] = block[:, 0:lanes]
        sums_ref[g, 1] = block[:, lanes : 2 * lanes] + block[:, 2 * lanes : 3 * lanes]
        for diagonal in range(planes - 2):
            piece = block[:, (diagonal + 3) * lanes : (diagonal + 4) * lanes]
            res_ref[g, diagonal] = piece.astype(jnp.bfloat16)


def coadd(targets, rows):
    sources, planes, row_count, lanes = rows.shape
    return pl.pallas_call(
        coadd_kernel,
        out_shape=(
            jax.ShapeDtypeStruct((ZS, 2, QROWS, lanes), jnp.float32),
            jax.ShapeDtypeStruct((ZS, planes - 2, QROWS, lanes), jnp.bfloat16),
        ),
        grid=(ZS // GROUP,),
        in_specs=[
            pl.BlockSpec((1, sources * row_count), lambda i: (0, 0)),
            pl.BlockSpec(rows.shape, lambda i: (0, 0, 0, 0)),
        ],
        out_specs=(
            pl.BlockSpec((GROUP, 2, QROWS, lanes), lambda i: (i, 0, 0, 0)),
            pl.BlockSpec((GROUP, planes - 2, QROWS, lanes), lambda i: (i, 0, 0, 0)),
        ),
        scratch_shapes=[pltpu.VMEM((sources * row_count, (planes + 1) * lanes), jnp.bfloat16)],
        compiler_params=pltpu.CompilerParams(vmem_limit_bytes=56 << 20),
        cost_estimate=pl.CostEstimate(
            flops=2 * ZS * QROWS * sources * row_count * (planes + 1) * lanes,
            bytes_accessed=2 * (rows.size + ZS * QROWS * planes * lanes),
            transcendentals=0,
        ),
    )(targets, rows)


def shards(
    exposure_flux,
    exposure_ivar,
    exposure_res,
    target_of_row,
    valid_of_row,
    rest_basis,
    redshift_shift,
):
    device = lax.axis_index("tgt")
    my_z = (device // CS) % ZS
    row_count, wave_dev = exposure_flux.shape
    lanes = wave_dev // PLANE
    outgoing = pack(exposure_ivar, exposure_flux, jnp.transpose(exposure_res, (1, 0, 2)))
    rows = lax.all_to_all(
        outgoing, "tgt", split_axis=0, concat_axis=0, axis_index_groups=plane_groups, tiled=True
    )
    masked = jnp.where(valid_of_row == 1, target_of_row, -1).reshape(XS, ZS, CS * row_count)
    targets = lax.dynamic_index_in_dim(masked, my_z, 1, keepdims=False).reshape(1, -1)
    part_sums, part_res = coadd(targets, rows)

    res_sum = lax.psum_scatter(
        part_res, "tgt", scatter_dimension=0, axis_index_groups=ring_groups, tiled=False
    )

    def part(offset):
        return lax.dynamic_index_in_dim(part_sums, (my_z + offset) % ZS, 0, keepdims=False)

    half = ZS // 2
    up, down = part(half), part(half + 1)
    for s in range(half):
        up = ring_step(up, 1)
        if s < half - 1:
            up = up + part(half - 1 - s)
            down = ring_step(down, -1)
            if s < half - 2:
                down = down + part(half + 2 + s)
    sums = part(0) + up + down

    def to_owner(values):
        kinds = values.shape[0]
        split = jnp.transpose(values.reshape(kinds, PLANE, TGT_DEV, lanes), (1, 0, 2, 3))
        back = lax.all_to_all(
            split, "tgt", split_axis=0, concat_axis=0, axis_index_groups=plane_groups, tiled=True
        )
        return jnp.transpose(back, (1, 2, 0, 3)).reshape(kinds, TGT_DEV, wave_dev)

    own = to_owner(sums)
    everything = lax.all_gather(own.astype(jnp.bfloat16), "band", axis=2, tiled=True)
    everything = everything.astype(jnp.float32)
    own_weight = own[0]
    coadd_flux = own[1] / own_weight
    band_index = lax.axis_index("band")
    shifts = lax.dynamic_slice_in_dim(redshift_shift, band_index * Z_DEV, Z_DEV)
    windows = basis_windows(rest_basis, shifts, 0, everything.shape[2])
    fit_gain = fit_from(*normal_terms(everything[0], everything[1], windows))

    own_res = to_owner(res_sum).astype(jnp.float32)
    coadd_res = jnp.transpose((own_res / own_weight[None]).astype(jnp.bfloat16), (1, 0, 2))
    return (coadd_flux, coadd_res, fit_gain)


def solution(mesh):
    in_specs = (P("tgt", "band"), P("tgt", "band"), P("tgt", None, "band"), P(), P(), P(), P())
    out_specs = (P("tgt", "band"), P("tgt", None, "band"), P("tgt", "band"))
    return jax.shard_map(shards, mesh=mesh, in_specs=in_specs, out_specs=out_specs, check_vma=False)
```

```python
import jax
import jax.numpy as jnp
import numpy as np
from jax import lax
from jax.experimental import pallas as pl
from jax.experimental.pallas import tpu as pltpu
from jax.sharding import PartitionSpec as P

TGT_DEV = 16
NDIAG = 11
Z_DEV = 8

XS, ZS, CS = 4, 16, 2
PLANE = XS * CS
QROWS = PLANE * TGT_DEV


def place(x, z, c):
    return ((x % XS) * ZS + z % ZS) * CS + c % CS


plane_groups = [[place(x, z, c) for x in range(XS) for c in range(CS)] for z in range(ZS)]
ring_groups = [[place(x, z, c) for z in range(ZS)] for x in range(XS) for c in range(CS)]


def ring_step(values, step):
    pairs = [
        (place(x, z, c), place(x, z + step, c))
        for x in range(XS)
        for z in range(ZS)
        for c in range(CS)
    ]
    return lax.ppermute(values, "tgt", pairs)


pair_first, pair_second = np.triu_indices(10)


def solve_normal(matrix, right_side):
    basis_count = right_side.shape[0]
    rows_of = [[None] * basis_count for column in range(basis_count)]
    for p in range(len(pair_first)):
        b = int(pair_first[p])
        c = int(pair_second[p])
        rows_of[b][c] = matrix[p]
        rows_of[c][b] = matrix[p]
    vector = [right_side[b] for b in range(basis_count)]
    for k in range(basis_count):
        inverse = 1.0 / rows_of[k][k]
        for r in range(k + 1, basis_count):
            factor = rows_of[r][k] * inverse
            for c in range(k + 1, basis_count):
                rows_of[r][c] = rows_of[r][c] - factor * rows_of[k][c]
            vector[r] = vector[r] - factor * vector[k]
    answer = [None] * basis_count
    for k in reversed(range(basis_count)):
        running = vector[k]
        for c in range(k + 1, basis_count):
            running = running - rows_of[k][c] * answer[c]
        answer[k] = running / rows_of[k][k]
    gain_total = right_side[0] * answer[0]
    for b in range(1, basis_count):
        gain_total = gain_total + right_side[b] * answer[b]
    return gain_total


def basis_windows(rest_basis, shifts, first_wave, length):

    def one_shift(shift_value):
        return lax.dynamic_slice_in_dim(rest_basis, first_wave + shift_value, length, axis=1)

    return jax.vmap(one_shift)(shifts)


def normal_terms(weight_sum, flux_sum, windows):
    products = windows[:, pair_first, :] * windows[:, pair_second, :]
    matrix = jnp.einsum("ti,zpi->ztp", weight_sum, products, precision=lax.Precision.HIGHEST)
    right_side = jnp.einsum("ti,zbi->ztb", flux_sum, windows, precision=lax.Precision.HIGHEST)
    return (matrix, right_side)


def fit_from(matrix, right_side):
    pairs = jnp.transpose(matrix, (2, 0, 1)).reshape(matrix.shape[2], -1)
    sides = jnp.transpose(right_side, (2, 0, 1)).reshape(right_side.shape[2], -1)
    gain = solve_normal(pairs, sides).reshape(matrix.shape[0], matrix.shape[1])
    return gain.T


GROUP = 4


def split_lanes_kernel(source_ref, out_ref):
    lanes = out_ref.shape[-1]
    for part in range(PLANE):
        out_ref[part] = source_ref[:, :, part * lanes : (part + 1) * lanes]


def split_lanes(values):
    planes, row_count, wave_dev = values.shape
    lanes = wave_dev // PLANE
    return pl.pallas_call(
        split_lanes_kernel,
        out_shape=jax.ShapeDtypeStruct((PLANE, planes, row_count, lanes), values.dtype),
        grid=(planes,),
        in_specs=[pl.BlockSpec((1, row_count, wave_dev), lambda i: (i, 0, 0))],
        out_specs=pl.BlockSpec((PLANE, 1, row_count, lanes), lambda i: (0, i, 0, 0)),
        cost_estimate=pl.CostEstimate(
            flops=0, bytes_accessed=4 * planes * row_count * wave_dev, transcendentals=0
        ),
    )(values)


def split_pair_kernel(ivar_ref, flux_ref, out_ref):
    lanes = out_ref.shape[-1]
    for part in range(PLANE):
        out_ref[part, 0] = ivar_ref[:, part * lanes : (part + 1) * lanes]
        out_ref[part, 1] = flux_ref[:, part * lanes : (part + 1) * lanes]


def split_pair(ivar, flux):
    row_count, wave_dev = ivar.shape
    lanes = wave_dev // PLANE
    return pl.pallas_call(
        split_pair_kernel,
        out_shape=jax.ShapeDtypeStruct((PLANE, 2, row_count, lanes), ivar.dtype),
        cost_estimate=pl.CostEstimate(
            flops=0, bytes_accessed=8 * row_count * wave_dev, transcendentals=0
        ),
    )(ivar, flux)


def members(target_ref, step):
    per_x = CS * TGT_DEV
    local = lax.broadcasted_iota(jnp.int32, (GROUP * QROWS, 1), 0)
    q = local % QROWS
    plane_z = step * GROUP + local // QROWS
    wanted = (q // per_x) * (ZS * per_x) + plane_z * per_x + q % per_x
    return jnp.where(target_ref[...] == wanted, 1.0, 0.0).astype(jnp.bfloat16)


def pair_kernel(target_ref, rows_ref, sums_ref, terms):
    sources, planes, row_count, lanes = rows_ref.shape
    step = pl.program_id(0)

    @pl.when(step == 0)
    def fill_terms():
        for source in range(sources):
            rows = slice(source * row_count, (source + 1) * row_count)
            weight = rows_ref[source, 0].astype(jnp.float32)
            terms[rows, 0:lanes] = rows_ref[source, 0]
            product = weight * rows_ref[source, 1].astype(jnp.float32)
            rounded = product.astype(jnp.bfloat16)
            terms[rows, lanes : 2 * lanes] = rounded
            rest = product - rounded.astype(jnp.float32)
            terms[rows, 2 * lanes : 3 * lanes] = rest.astype(jnp.bfloat16)

    sums = jnp.dot(members(target_ref, step), terms[...], preferred_element_type=jnp.float32)
    for g in range(GROUP):
        block = sums[g * QROWS : (g + 1) * QROWS]
        sums_ref[g, 0] = block[:, 0:lanes]
        sums_ref[g, 1] = block[:, lanes : 2 * lanes] + block[:, 2 * lanes : 3 * lanes]


def coadd_pair(targets, rows):
    sources, planes, row_count, lanes = rows.shape
    return pl.pallas_call(
        pair_kernel,
        out_shape=jax.ShapeDtypeStruct((ZS, 2, QROWS, lanes), jnp.float32),
        grid=(ZS // GROUP,),
        in_specs=[
            pl.BlockSpec((1, sources * row_count), lambda i: (0, 0)),
            pl.BlockSpec(rows.shape, lambda i: (0, 0, 0, 0)),
        ],
        out_specs=pl.BlockSpec((GROUP, 2, QROWS, lanes), lambda i: (i, 0, 0, 0)),
        scratch_shapes=[pltpu.VMEM((sources * row_count, 3 * lanes), jnp.bfloat16)],
        compiler_params=pltpu.CompilerParams(vmem_limit_bytes=40 << 20),
        cost_estimate=pl.CostEstimate(
            flops=2 * ZS * QROWS * sources * row_count * 3 * lanes,
            bytes_accessed=2 * rows.size + 8 * ZS * QROWS * lanes,
            transcendentals=0,
        ),
    )(targets, rows)


def res_kernel(target_ref, pair_ref, rows_ref, res_ref, terms):
    sources, planes, row_count, lanes = rows_ref.shape
    step = pl.program_id(0)

    @pl.when(step == 0)
    def fill_terms():
        def one_source(source, carry):
            rows = pl.ds(pl.multiple_of(source * row_count, row_count), row_count)
            weight = pair_ref[source, 0].astype(jnp.float32)
            for plane in range(planes):
                product = weight * rows_ref[source, plane].astype(jnp.float32)
                terms[rows, plane * lanes : (plane + 1) * lanes] = product.astype(jnp.bfloat16)
            return carry

        lax.fori_loop(0, sources, one_source, 0)

    sums = jnp.dot(members(target_ref, step), terms[...], preferred_element_type=jnp.float32)
    for g in range(GROUP):
        for owner in range(PLANE):
            first = g * QROWS + owner * TGT_DEV
            block = sums[first : first + TGT_DEV].astype(jnp.bfloat16)
            for diagonal in range(planes):
                res_ref[g, owner, diagonal] = block[:, diagonal * lanes : (diagonal + 1) * lanes]


def coadd_res_rows(targets, pair, rows):
    sources, planes, row_count, lanes = rows.shape
    return pl.pallas_call(
        res_kernel,
        out_shape=jax.ShapeDtypeStruct((ZS, PLANE, planes, TGT_DEV, lanes), jnp.bfloat16),
        grid=(ZS // GROUP,),
        in_specs=[
            pl.BlockSpec((1, sources * row_count), lambda i: (0, 0)),
            pl.BlockSpec(pair.shape, lambda i: (0, 0, 0, 0)),
            pl.BlockSpec(rows.shape, lambda i: (0, 0, 0, 0)),
        ],
        out_specs=pl.BlockSpec(
            (GROUP, PLANE, planes, TGT_DEV, lanes), lambda i: (i, 0, 0, 0, 0)
        ),
        scratch_shapes=[pltpu.VMEM((sources * row_count, planes * lanes), jnp.bfloat16)],
        compiler_params=pltpu.CompilerParams(vmem_limit_bytes=56 << 20),
        cost_estimate=pl.CostEstimate(
            flops=2 * ZS * QROWS * sources * row_count * planes * lanes,
            bytes_accessed=2 * (rows.size + ZS * QROWS * planes * lanes),
            transcendentals=0,
        ),
    )(targets, pair, rows)


def exchange(values):
    return lax.all_to_all(
        values, "tgt", split_axis=0, concat_axis=0, axis_index_groups=plane_groups, tiled=True
    )


def scatter_sum(values):
    return lax.psum_scatter(
        values, "tgt", scatter_dimension=0, axis_index_groups=ring_groups, tiled=False
    )


def ring_sum(parts, my_z):
    def part(offset):
        return lax.dynamic_index_in_dim(parts, (my_z + offset) % ZS, 0, keepdims=False)

    half = ZS // 2
    up, down = part(half), part(half + 1)
    for s in range(half):
        up = ring_step(up, 1)
        if s < half - 1:
            up = up + part(half - 1 - s)
            down = ring_step(down, -1)
            if s < half - 2:
                down = down + part(half + 2 + s)
    return part(0) + up + down


def shards(
    exposure_flux,
    exposure_ivar,
    exposure_res,
    target_of_row,
    valid_of_row,
    rest_basis,
    redshift_shift,
):
    device = lax.axis_index("tgt")
    my_z = (device // CS) % ZS
    row_count, wave_dev = exposure_flux.shape
    lanes = wave_dev // PLANE
    masked = jnp.where(valid_of_row == 1, target_of_row, -1).reshape(XS, ZS, CS * row_count)
    targets = lax.dynamic_index_in_dim(masked, my_z, 1, keepdims=False).reshape(1, -1)

    pair = exchange(split_pair(exposure_ivar, exposure_flux))
    packed = split_lanes(jnp.transpose(exposure_res, (1, 0, 2)))
    packed, pair = lax.optimization_barrier((packed, pair))
    rows = exchange(packed)
    sums = ring_sum(coadd_pair(targets, pair), my_z)
    rows, sums = lax.optimization_barrier((rows, sums))
    res_sum = scatter_sum(coadd_res_rows(targets, pair, rows))

    split = jnp.transpose(sums.reshape(2, PLANE, TGT_DEV, lanes), (1, 0, 2, 3))
    own = jnp.transpose(exchange(split), (1, 2, 0, 3)).reshape(2, TGT_DEV, wave_dev)
    everything = lax.all_gather(own.astype(jnp.bfloat16), "band", axis=2, tiled=True)
    everything = everything.astype(jnp.float32)
    coadd_flux = own[1] / own[0]
    band_index = lax.axis_index("band")
    shifts = lax.dynamic_slice_in_dim(redshift_shift, band_index * Z_DEV, Z_DEV)
    windows = basis_windows(rest_basis, shifts, 0, everything.shape[2])
    fit_gain = fit_from(*normal_terms(everything[0], everything[1], windows))

    back = exchange(res_sum)
    own_res = jnp.transpose(back, (1, 2, 0, 3)).reshape(NDIAG, TGT_DEV, wave_dev)
    coadd_res = (own_res.astype(jnp.float32) / own[0][None]).astype(jnp.bfloat16)
    return (coadd_flux, jnp.transpose(coadd_res, (1, 0, 2)), fit_gain)


def solution(mesh):
    in_specs = (P("tgt", "band"), P("tgt", "band"), P("tgt", None, "band"), P(), P(), P(), P())
    out_specs = (P("tgt", "band"), P("tgt", None, "band"), P("tgt", "band"))
    return jax.shard_map(shards, mesh=mesh, in_specs=in_specs, out_specs=out_specs, check_vma=False)
```

```python
import jax
import jax.numpy as jnp
import numpy as np
from jax import lax
from jax.experimental import pallas as pl
from jax.experimental.pallas import tpu as pltpu
from jax.sharding import PartitionSpec as P

TGT_DEV = 16
NDIAG = 11
Z_DEV = 8

XS, ZS, CS = 4, 16, 2
PLANE = XS * CS
QROWS = PLANE * TGT_DEV


def place(x, z, c):
    return ((x % XS) * ZS + z % ZS) * CS + c % CS


plane_groups = [[place(x, z, c) for x in range(XS) for c in range(CS)] for z in range(ZS)]
PAIR = 2
STATIONS = ZS // PAIR
WIDE = PLANE * PAIR
wide_groups = [
    [place(x, h * PAIR + p, c) for x in range(XS) for p in range(PAIR) for c in range(CS)]
    for h in range(STATIONS)
]
ring_groups = [[place(x, z, c) for z in range(ZS)] for x in range(XS) for c in range(CS)]


def ring_step(values, step):
    pairs = [
        (place(x, z, c), place(x, z + step * PAIR, c))
        for x in range(XS)
        for z in range(ZS)
        for c in range(CS)
    ]
    return lax.ppermute(values, "tgt", pairs)


pair_first, pair_second = np.triu_indices(10)


def solve_normal(matrix, right_side):
    basis_count = right_side.shape[0]
    rows_of = [[None] * basis_count for column in range(basis_count)]
    for p in range(len(pair_first)):
        b = int(pair_first[p])
        c = int(pair_second[p])
        rows_of[b][c] = matrix[p]
        rows_of[c][b] = matrix[p]
    vector = [right_side[b] for b in range(basis_count)]
    for k in range(basis_count):
        inverse = 1.0 / rows_of[k][k]
        for r in range(k + 1, basis_count):
            factor = rows_of[r][k] * inverse
            for c in range(k + 1, basis_count):
                rows_of[r][c] = rows_of[r][c] - factor * rows_of[k][c]
            vector[r] = vector[r] - factor * vector[k]
    answer = [None] * basis_count
    for k in reversed(range(basis_count)):
        running = vector[k]
        for c in range(k + 1, basis_count):
            running = running - rows_of[k][c] * answer[c]
        answer[k] = running / rows_of[k][k]
    gain_total = right_side[0] * answer[0]
    for b in range(1, basis_count):
        gain_total = gain_total + right_side[b] * answer[b]
    return gain_total


def basis_windows(rest_basis, shifts, first_wave, length):

    def one_shift(shift_value):
        return lax.dynamic_slice_in_dim(rest_basis, first_wave + shift_value, length, axis=1)

    return jax.vmap(one_shift)(shifts)


def normal_terms(weight_sum, flux_sum, windows):
    products = windows[:, pair_first, :] * windows[:, pair_second, :]
    matrix = jnp.einsum("ti,zpi->ztp", weight_sum, products, precision=lax.Precision.HIGHEST)
    right_side = jnp.einsum("ti,zbi->ztb", flux_sum, windows, precision=lax.Precision.HIGHEST)
    return (matrix, right_side)


def fit_from(matrix, right_side):
    pairs = jnp.transpose(matrix, (2, 0, 1)).reshape(matrix.shape[2], -1)
    sides = jnp.transpose(right_side, (2, 0, 1)).reshape(right_side.shape[2], -1)
    gain = solve_normal(pairs, sides).reshape(matrix.shape[0], matrix.shape[1])
    return gain.T


GROUP = 4


def split_kernel(ivar_ref, res_ref, out_ref):
    lanes = out_ref.shape[-1]
    for part in range(PLANE):
        columns = slice(part * lanes, (part + 1) * lanes)
        out_ref[part, 0] = ivar_ref[:, columns]
        out_ref[part, 1:] = res_ref[:, :, columns]


def split_lanes(ivar, res):
    diagonals, row_count, wave_dev = res.shape
    lanes = wave_dev // PLANE
    return pl.pallas_call(
        split_kernel,
        out_shape=jax.ShapeDtypeStruct((PLANE, diagonals + 1, row_count, lanes), res.dtype),
        compiler_params=pltpu.CompilerParams(vmem_limit_bytes=40 << 20),
        cost_estimate=pl.CostEstimate(
            flops=0, bytes_accessed=4 * (diagonals + 1) * row_count * wave_dev, transcendentals=0
        ),
    )(ivar, res)


def members(target_ref, step):
    per_x = CS * TGT_DEV
    local = lax.broadcasted_iota(jnp.int32, (GROUP * QROWS, 1), 0)
    q = local % QROWS
    plane_z = step * GROUP + local // QROWS
    wanted = (q // per_x) * (ZS * per_x) + plane_z * per_x + q % per_x
    return jnp.where(target_ref[...] == wanted, 1.0, 0.0).astype(jnp.bfloat16)


def res_kernel(target_ref, rows_ref, res_ref, terms):
    sources, planes, row_count, lanes = rows_ref.shape
    step = pl.program_id(0)

    @pl.when(step == 0)
    def fill_terms():
        def one_source(source, carry):
            rows = pl.ds(pl.multiple_of(source * row_count, row_count), row_count)
            weight = rows_ref[source, 0].astype(jnp.float32)
            for plane in range(1, planes):
                product = weight * rows_ref[source, plane].astype(jnp.float32)
                terms[rows, (plane - 1) * lanes : plane * lanes] = product.astype(jnp.bfloat16)
            return carry

        lax.fori_loop(0, sources, one_source, 0)

    sums = jnp.dot(members(target_ref, step), terms[...], preferred_element_type=jnp.float32)
    for g in range(GROUP):
        for owner in range(PLANE):
            first = g * QROWS + owner * TGT_DEV
            block = sums[first : first + TGT_DEV].astype(jnp.bfloat16)
            for diagonal in range(planes - 1):
                res_ref[g, owner, diagonal] = block[:, diagonal * lanes : (diagonal + 1) * lanes]


def coadd_res_rows(targets, rows):
    sources, planes, row_count, lanes = rows.shape
    out_shape = (ZS, PLANE, planes - 1, TGT_DEV, lanes)
    return pl.pallas_call(
        res_kernel,
        out_shape=jax.ShapeDtypeStruct(out_shape, jnp.bfloat16),
        grid=(ZS // GROUP,),
        in_specs=[
            pl.BlockSpec((1, sources * row_count), lambda i: (0, 0)),
            pl.BlockSpec(rows.shape, lambda i: (0, 0, 0, 0)),
        ],
        out_specs=pl.BlockSpec((GROUP,) + out_shape[1:], lambda i: (i, 0, 0, 0, 0)),
        scratch_shapes=[pltpu.VMEM((sources * row_count, (planes - 1) * lanes), jnp.bfloat16)],
        compiler_params=pltpu.CompilerParams(vmem_limit_bytes=56 << 20),
        cost_estimate=pl.CostEstimate(
            flops=2 * ZS * QROWS * sources * row_count * (planes - 1) * lanes,
            bytes_accessed=2 * (rows.size + ZS * QROWS * planes * lanes),
            transcendentals=0,
        ),
    )(targets, rows)


def half_swap(values):
    return pltpu.roll(values, values.shape[-1] // 2, 1)


def mix_kernel(ivar_ref, flux_ref, out_ref):
    row_count, lanes = out_ref.shape[1:]
    first = lax.broadcasted_iota(jnp.int32, (row_count, lanes), 1) < lanes // 2
    for tile in range(WIDE // 2):
        columns = slice(tile * lanes, (tile + 1) * lanes)
        ivar = ivar_ref[:, columns].astype(jnp.float32)
        flux = flux_ref[:, columns].astype(jnp.float32)
        low = jnp.where(first, ivar, half_swap(flux))
        high = jnp.where(first, half_swap(ivar), flux)
        out_ref[2 * tile] = low.astype(out_ref.dtype)
        out_ref[2 * tile + 1] = high.astype(out_ref.dtype)


def mix_pair(ivar, flux):
    row_count, wave_dev = ivar.shape
    return pl.pallas_call(
        mix_kernel,
        out_shape=jax.ShapeDtypeStruct((WIDE, row_count, 2 * wave_dev // WIDE), ivar.dtype),
        cost_estimate=pl.CostEstimate(
            flops=0, bytes_accessed=8 * row_count * wave_dev, transcendentals=0
        ),
    )(ivar, flux)


BATCH = 2


def mix_sum_kernel(target_ref, rows_ref, sums_ref, terms):
    sources, row_count, lanes = rows_ref.shape
    block_rows = WIDE * TGT_DEV
    step = pl.program_id(0)

    @pl.when(step == 0)
    def fill_terms():
        first = lax.broadcasted_iota(jnp.int32, (row_count, lanes), 1) < lanes // 2
        for source in range(sources):
            rows = slice(source * row_count, (source + 1) * row_count)
            values = rows_ref[source].astype(jnp.float32)
            product = jnp.where(first, values, values * half_swap(values))
            rounded = product.astype(jnp.bfloat16)
            terms[rows, 0:lanes] = rounded
            rest = product - rounded.astype(jnp.float32)
            terms[rows, lanes : 2 * lanes] = rest.astype(jnp.bfloat16)

    per_x = PAIR * CS * TGT_DEV
    local = lax.broadcasted_iota(jnp.int32, (BATCH * block_rows, 1), 0)
    q = local % block_rows
    station = step * BATCH + local // block_rows
    wanted = (q // per_x) * (STATIONS * per_x) + station * per_x + q % per_x
    member = jnp.where(target_ref[...] == wanted, 1.0, 0.0).astype(jnp.bfloat16)
    sums = jnp.dot(member, terms[...], preferred_element_type=jnp.float32)
    total = sums[:, 0:lanes] + sums[:, lanes : 2 * lanes]
    for b in range(BATCH):
        sums_ref[b] = total[b * block_rows : (b + 1) * block_rows]


def mix_sum(targets, rows):
    sources, row_count, lanes = rows.shape
    block_rows = WIDE * TGT_DEV
    return pl.pallas_call(
        mix_sum_kernel,
        out_shape=jax.ShapeDtypeStruct((STATIONS, block_rows, lanes), jnp.float32),
        grid=(STATIONS // BATCH,),
        in_specs=[
            pl.BlockSpec((1, sources * row_count), lambda i: (0, 0)),
            pl.BlockSpec(rows.shape, lambda i: (0, 0, 0)),
        ],
        out_specs=pl.BlockSpec((BATCH, block_rows, lanes), lambda i: (i, 0, 0)),
        scratch_shapes=[pltpu.VMEM((sources * row_count, 2 * lanes), jnp.bfloat16)],
        compiler_params=pltpu.CompilerParams(vmem_limit_bytes=40 << 20),
        cost_estimate=pl.CostEstimate(
            flops=4 * STATIONS * block_rows * sources * row_count * lanes,
            bytes_accessed=2 * rows.size + 4 * STATIONS * block_rows * lanes,
            transcendentals=0,
        ),
    )(targets, rows)


def ring_sum(parts, station):
    def part(offset):
        return lax.dynamic_index_in_dim(parts, (station + offset) % STATIONS, 0, keepdims=False)

    half = STATIONS // 2
    up, down = part(half), part(half + 1)
    for s in range(half):
        up = ring_step(up, 1)
        if s < half - 1:
            up = up + part(half - 1 - s)
            down = ring_step(down, -1)
            if s < half - 2:
                down = down + part(half + 2 + s)
    return part(0) + up + down


def exchange(values, groups):
    return lax.all_to_all(
        values, "tgt", split_axis=0, concat_axis=0, axis_index_groups=groups, tiled=True
    )


def scatter_sum(values):
    return lax.psum_scatter(
        values, "tgt", scatter_dimension=0, axis_index_groups=ring_groups, tiled=False
    )


def shards(
    exposure_flux,
    exposure_ivar,
    exposure_res,
    target_of_row,
    valid_of_row,
    rest_basis,
    redshift_shift,
):
    device = lax.axis_index("tgt")
    my_z = (device // CS) % ZS
    row_count, wave_dev = exposure_flux.shape
    masked = jnp.where(valid_of_row == 1, target_of_row, -1)
    targets = lax.dynamic_index_in_dim(
        masked.reshape(XS, ZS, CS * row_count), my_z, 1, keepdims=False
    ).reshape(1, -1)
    wide_targets = lax.dynamic_index_in_dim(
        masked.reshape(XS, STATIONS, PAIR * CS * row_count), my_z // PAIR, 1, keepdims=False
    ).reshape(1, -1)

    mixed = exchange(mix_pair(exposure_ivar, exposure_flux), wide_groups)
    packed = split_lanes(exposure_ivar, jnp.transpose(exposure_res, (1, 0, 2)))
    packed, mixed = lax.optimization_barrier((packed, mixed))
    rows = exchange(packed, plane_groups)
    sums = ring_sum(mix_sum(wide_targets, mixed), my_z // PAIR)
    rows, sums = lax.optimization_barrier((rows, sums))
    res_sum = scatter_sum(coadd_res_rows(targets, rows))

    own = exchange(sums.reshape(WIDE, TGT_DEV, -1), wide_groups)
    own = jnp.transpose(own.reshape(WIDE, TGT_DEV, 2, wave_dev // WIDE), (2, 1, 0, 3))
    own = own.reshape(2, TGT_DEV, wave_dev)
    everything = lax.all_gather(own.astype(jnp.bfloat16), "band", axis=2, tiled=True)
    everything = everything.astype(jnp.float32)
    coadd_flux = own[1] / own[0]
    band_index = lax.axis_index("band")
    shifts = lax.dynamic_slice_in_dim(redshift_shift, band_index * Z_DEV, Z_DEV)
    windows = basis_windows(rest_basis, shifts, 0, everything.shape[2])
    fit_gain = fit_from(*normal_terms(everything[0], everything[1], windows))

    back = exchange(res_sum, plane_groups)
    own_res = jnp.transpose(back, (1, 2, 0, 3)).reshape(NDIAG, TGT_DEV, wave_dev)
    coadd_res = (own_res.astype(jnp.float32) / own[0][None]).astype(jnp.bfloat16)
    return (coadd_flux, jnp.transpose(coadd_res, (1, 0, 2)), fit_gain)


def solution(mesh):
    in_specs = (P("tgt", "band"), P("tgt", "band"), P("tgt", None, "band"), P(), P(), P(), P())
    out_specs = (P("tgt", "band"), P("tgt", None, "band"), P("tgt", "band"))
    return jax.shard_map(shards, mesh=mesh, in_specs=in_specs, out_specs=out_specs, check_vma=False)
```

```python
import jax
import jax.numpy as jnp
import numpy as np
from jax import lax
from jax.experimental import pallas as pl
from jax.experimental.pallas import tpu as pltpu
from jax.sharding import PartitionSpec as P

TGT_DEV = 16
NDIAG = 11
Z_DEV = 8

XS, ZS, CS = 4, 16, 2
PLANE = XS * CS
QROWS = PLANE * TGT_DEV


def place(x, z, c):
    return ((x % XS) * ZS + z % ZS) * CS + c % CS


plane_groups = [[place(x, z, c) for x in range(XS) for c in range(CS)] for z in range(ZS)]
PAIR = 2
STATIONS = ZS // PAIR
WIDE = PLANE * PAIR
wide_groups = [
    [place(x, h * PAIR + p, c) for x in range(XS) for p in range(PAIR) for c in range(CS)]
    for h in range(STATIONS)
]
ring_groups = [[place(x, z, c) for z in range(ZS)] for x in range(XS) for c in range(CS)]


def ring_step(values, step):
    pairs = [
        (place(x, z, c), place(x, z + step * PAIR, c))
        for x in range(XS)
        for z in range(ZS)
        for c in range(CS)
    ]
    return lax.ppermute(values, "tgt", pairs)


pair_first, pair_second = np.triu_indices(10)


def solve_normal(matrix, right_side):
    basis_count = right_side.shape[0]
    rows_of = [[None] * basis_count for column in range(basis_count)]
    for p in range(len(pair_first)):
        b = int(pair_first[p])
        c = int(pair_second[p])
        rows_of[b][c] = matrix[p]
        rows_of[c][b] = matrix[p]
    vector = [right_side[b] for b in range(basis_count)]
    for k in range(basis_count):
        inverse = 1.0 / rows_of[k][k]
        for r in range(k + 1, basis_count):
            factor = rows_of[r][k] * inverse
            for c in range(k + 1, basis_count):
                rows_of[r][c] = rows_of[r][c] - factor * rows_of[k][c]
            vector[r] = vector[r] - factor * vector[k]
    answer = [None] * basis_count
    for k in reversed(range(basis_count)):
        running = vector[k]
        for c in range(k + 1, basis_count):
            running = running - rows_of[k][c] * answer[c]
        answer[k] = running / rows_of[k][k]
    gain_total = right_side[0] * answer[0]
    for b in range(1, basis_count):
        gain_total = gain_total + right_side[b] * answer[b]
    return gain_total


def basis_windows(rest_basis, shifts, first_wave, length):

    def one_shift(shift_value):
        return lax.dynamic_slice_in_dim(rest_basis, first_wave + shift_value, length, axis=1)

    return jax.vmap(one_shift)(shifts)


def normal_terms(weight_sum, flux_sum, windows):
    products = windows[:, pair_first, :] * windows[:, pair_second, :]
    matrix = jnp.einsum("ti,zpi->ztp", weight_sum, products, precision=lax.Precision.HIGHEST)
    right_side = jnp.einsum("ti,zbi->ztb", flux_sum, windows, precision=lax.Precision.HIGHEST)
    return (matrix, right_side)


def fit_from(matrix, right_side):
    pairs = jnp.transpose(matrix, (2, 0, 1)).reshape(matrix.shape[2], -1)
    sides = jnp.transpose(right_side, (2, 0, 1)).reshape(right_side.shape[2], -1)
    gain = solve_normal(pairs, sides).reshape(matrix.shape[0], matrix.shape[1])
    return gain.T


def half_swap(values):
    return pltpu.roll(values, values.shape[-1] // 2, 1)


def mix_kernel(ivar_ref, flux_ref, out_ref):
    row_count, lanes = out_ref.shape[1:]
    first = lax.broadcasted_iota(jnp.int32, (row_count, lanes), 1) < lanes // 2
    for tile in range(WIDE // 2):
        columns = slice(tile * lanes, (tile + 1) * lanes)
        ivar = ivar_ref[:, columns].astype(jnp.float32)
        flux = flux_ref[:, columns].astype(jnp.float32)
        low = jnp.where(first, ivar, half_swap(flux))
        high = jnp.where(first, half_swap(ivar), flux)
        out_ref[2 * tile] = low.astype(out_ref.dtype)
        out_ref[2 * tile + 1] = high.astype(out_ref.dtype)


def mix_pair(ivar, flux):
    row_count, wave_dev = ivar.shape
    return pl.pallas_call(
        mix_kernel,
        out_shape=jax.ShapeDtypeStruct((WIDE, row_count, 2 * wave_dev // WIDE), ivar.dtype),
        cost_estimate=pl.CostEstimate(
            flops=0, bytes_accessed=8 * row_count * wave_dev, transcendentals=0
        ),
    )(ivar, flux)


FOLDS = (NDIAG + 1) // 2


def mix_res_kernel(res_ref, out_ref):
    row_count, lanes = out_ref.shape[2:]
    first = lax.broadcasted_iota(jnp.int32, (row_count, lanes), 1) < lanes // 2
    for fold in range(FOLDS):
        for tile in range(WIDE // 2):
            columns = slice(tile * lanes, (tile + 1) * lanes)
            one = res_ref[2 * fold, :, columns].astype(jnp.float32)
            if 2 * fold + 1 < NDIAG:
                two = res_ref[2 * fold + 1, :, columns].astype(jnp.float32)
            else:
                two = jnp.zeros_like(one)
            low = jnp.where(first, one, half_swap(two))
            high = jnp.where(first, half_swap(one), two)
            out_ref[2 * tile, fold] = low.astype(out_ref.dtype)
            out_ref[2 * tile + 1, fold] = high.astype(out_ref.dtype)


def mix_res(res):
    diagonals, row_count, wave_dev = res.shape
    return pl.pallas_call(
        mix_res_kernel,
        out_shape=jax.ShapeDtypeStruct(
            (WIDE, FOLDS, row_count, 2 * wave_dev // WIDE), res.dtype
        ),
        compiler_params=pltpu.CompilerParams(vmem_limit_bytes=40 << 20),
        cost_estimate=pl.CostEstimate(
            flops=0, bytes_accessed=4 * (diagonals + 1) * row_count * wave_dev, transcendentals=0
        ),
    )(res)


BATCH = 2


def members(target_ref):
    block_rows = WIDE * TGT_DEV
    per_x = PAIR * CS * TGT_DEV
    local = lax.broadcasted_iota(jnp.int32, (BATCH * block_rows, 1), 0)
    q = local % block_rows
    station = pl.program_id(0) * BATCH + local // block_rows
    wanted = (q // per_x) * (STATIONS * per_x) + station * per_x + q % per_x
    return jnp.where(target_ref[...] == wanted, 1.0, 0.0).astype(jnp.bfloat16)


def mix_sum_kernel(target_ref, rows_ref, sums_ref, terms):
    sources, row_count, lanes = rows_ref.shape
    block_rows = WIDE * TGT_DEV

    @pl.when(pl.program_id(0) == 0)
    def fill_terms():
        first = lax.broadcasted_iota(jnp.int32, (row_count, lanes), 1) < lanes // 2
        for source in range(sources):
            rows = slice(source * row_count, (source + 1) * row_count)
            values = rows_ref[source].astype(jnp.float32)
            product = jnp.where(first, values, values * half_swap(values))
            rounded = product.astype(jnp.bfloat16)
            terms[rows, 0:lanes] = rounded
            rest = product - rounded.astype(jnp.float32)
            terms[rows, lanes : 2 * lanes] = rest.astype(jnp.bfloat16)

    sums = jnp.dot(members(target_ref), terms[...], preferred_element_type=jnp.float32)
    total = sums[:, 0:lanes] + sums[:, lanes : 2 * lanes]
    for b in range(BATCH):
        sums_ref[b] = total[b * block_rows : (b + 1) * block_rows]


def mix_sum(targets, rows):
    sources, row_count, lanes = rows.shape
    block_rows = WIDE * TGT_DEV
    return pl.pallas_call(
        mix_sum_kernel,
        out_shape=jax.ShapeDtypeStruct((STATIONS, block_rows, lanes), jnp.float32),
        grid=(STATIONS // BATCH,),
        in_specs=[
            pl.BlockSpec((1, sources * row_count), lambda i: (0, 0)),
            pl.BlockSpec(rows.shape, lambda i: (0, 0, 0)),
        ],
        out_specs=pl.BlockSpec((BATCH, block_rows, lanes), lambda i: (i, 0, 0)),
        scratch_shapes=[pltpu.VMEM((sources * row_count, 2 * lanes), jnp.bfloat16)],
        compiler_params=pltpu.CompilerParams(vmem_limit_bytes=40 << 20),
        cost_estimate=pl.CostEstimate(
            flops=4 * STATIONS * block_rows * sources * row_count * lanes,
            bytes_accessed=2 * rows.size + 4 * STATIONS * block_rows * lanes,
            transcendentals=0,
        ),
    )(targets, rows)


STREAMS = 2


def res_sum_kernel(target_ref, mixed_ref, rows_ref, *refs):
    sums_refs, terms = refs[:STREAMS], refs[STREAMS]
    sources, folds, row_count, lanes = rows_ref.shape
    block_rows = WIDE * TGT_DEV

    @pl.when(pl.program_id(0) == 0)
    def fill_terms():
        first = lax.broadcasted_iota(jnp.int32, (row_count, lanes), 1) < lanes // 2

        def one_source(source, carry):
            rows = pl.ds(pl.multiple_of(source * row_count, row_count), row_count)
            values = mixed_ref[source].astype(jnp.float32)
            weight = jnp.where(first, values, half_swap(values))
            for fold in range(folds):
                product = weight * rows_ref[source, fold].astype(jnp.float32)
                terms[rows, fold * lanes : (fold + 1) * lanes] = product.astype(jnp.bfloat16)
            return carry

        lax.fori_loop(0, sources, one_source, 0)

    sums = jnp.dot(members(target_ref), terms[...], preferred_element_type=jnp.float32)
    each = folds // STREAMS
    for b in range(BATCH):
        for owner in range(WIDE):
            start = b * block_rows + owner * TGT_DEV
            block = sums[start : start + TGT_DEV].astype(jnp.bfloat16)
            for fold in range(folds):
                piece = block[:, fold * lanes : (fold + 1) * lanes]
                sums_refs[fold // each][b, owner, fold % each] = piece


def res_sums(targets, mixed, rows):
    sources, folds, row_count, lanes = rows.shape
    tail = (WIDE, folds // STREAMS, TGT_DEV, lanes)
    return pl.pallas_call(
        res_sum_kernel,
        out_shape=[jax.ShapeDtypeStruct((STATIONS,) + tail, jnp.bfloat16)] * STREAMS,
        grid=(STATIONS // BATCH,),
        in_specs=[
            pl.BlockSpec((1, sources * row_count), lambda i: (0, 0)),
            pl.BlockSpec(mixed.shape, lambda i: (0, 0, 0)),
            pl.BlockSpec(rows.shape, lambda i: (0, 0, 0, 0)),
        ],
        out_specs=[pl.BlockSpec((BATCH,) + tail, lambda i: (i, 0, 0, 0, 0))] * STREAMS,
        scratch_shapes=[pltpu.VMEM((sources * row_count, folds * lanes), jnp.bfloat16)],
        compiler_params=pltpu.CompilerParams(vmem_limit_bytes=48 << 20),
        cost_estimate=pl.CostEstimate(
            flops=2 * STATIONS * WIDE * TGT_DEV * sources * row_count * folds * lanes,
            bytes_accessed=2 * (rows.size + STATIONS * WIDE * TGT_DEV * folds * lanes),
            transcendentals=0,
        ),
    )(targets, mixed, rows)


def unfold(low, high, first):
    one = jnp.where(first, low, half_swap(high))
    two = jnp.where(first, half_swap(low), high)
    return one, two


def own_kernel(sums_ref, weight_ref, coadd_ref, both_ref):
    lanes = sums_ref.shape[-1]
    first = lax.broadcasted_iota(jnp.int32, (TGT_DEV, lanes), 1) < lanes // 2
    for tile in range(WIDE // 2):
        columns = slice(tile * lanes, (tile + 1) * lanes)
        weight, flux = unfold(sums_ref[2 * tile], sums_ref[2 * tile + 1], first)
        weight_ref[:, columns] = weight
        coadd_ref[:, columns] = flux / weight
        both_ref[0, :, columns] = weight.astype(jnp.bfloat16)
        both_ref[1, :, columns] = flux.astype(jnp.bfloat16)


def own_sums(sums):
    wave_dev = WIDE * sums.shape[-1] // 2
    whole = jax.ShapeDtypeStruct((TGT_DEV, wave_dev), jnp.float32)
    both = jax.ShapeDtypeStruct((2, TGT_DEV, wave_dev), jnp.bfloat16)
    return pl.pallas_call(own_kernel, out_shape=(whole, whole, both))(sums)


def finish_kernel(weight_ref, *refs):
    sums_refs, out_ref = refs[:STREAMS], refs[STREAMS]
    each, lanes = sums_refs[0].shape[1], sums_refs[0].shape[-1]
    first = lax.broadcasted_iota(jnp.int32, (TGT_DEV, lanes), 1) < lanes // 2
    for tile in range(WIDE // 2):
        columns = slice(tile * lanes, (tile + 1) * lanes)
        weight = weight_ref[:, columns]
        for fold in range(FOLDS):
            low = sums_refs[fold // each][2 * tile, fold % each].astype(jnp.float32)
            high = sums_refs[fold // each][2 * tile + 1, fold % each].astype(jnp.float32)
            one, two = unfold(low, high, first)
            out_ref[2 * fold, :, columns] = (one / weight).astype(jnp.bfloat16)
            if 2 * fold + 1 < NDIAG:
                out_ref[2 * fold + 1, :, columns] = (two / weight).astype(jnp.bfloat16)


def finish(weight, sums):
    out = jax.ShapeDtypeStruct((NDIAG,) + weight.shape, jnp.bfloat16)
    return pl.pallas_call(finish_kernel, out_shape=out)(weight, *sums)


def ring_start(parts, station):
    def part(offset):
        return lax.dynamic_index_in_dim(parts, (station + offset) % STATIONS, 0, keepdims=False)

    return part, part(STATIONS // 2), part(STATIONS // 2 + 1)


def ring_turn(state, s):
    half = STATIONS // 2
    part, up, down = state
    up = ring_step(up, 1)
    if s < half - 1:
        up = up + part(half - 1 - s)
        down = ring_step(down, -1)
        if s < half - 2:
            down = down + part(half + 2 + s)
    return part, up, down


def ring_end(state):
    part, up, down = state
    total = part(0).astype(jnp.float32) + up.astype(jnp.float32) + down.astype(jnp.float32)
    return total.astype(up.dtype)


def exchange(values, groups):
    return lax.all_to_all(
        values, "tgt", split_axis=0, concat_axis=0, axis_index_groups=groups, tiled=True
    )


def shards(
    exposure_flux,
    exposure_ivar,
    exposure_res,
    target_of_row,
    valid_of_row,
    rest_basis,
    redshift_shift,
):
    device = lax.axis_index("tgt")
    my_z = (device // CS) % ZS
    row_count, wave_dev = exposure_flux.shape
    masked = jnp.where(valid_of_row == 1, target_of_row, -1)
    station = my_z // PAIR
    targets = lax.dynamic_index_in_dim(
        masked.reshape(XS, STATIONS, PAIR * CS * row_count), station, 1, keepdims=False
    ).reshape(1, -1)

    mixed = exchange(mix_pair(exposure_ivar, exposure_flux), wide_groups)
    packed = mix_res(jnp.transpose(exposure_res, (1, 0, 2)))
    packed, mixed = lax.optimization_barrier((packed, mixed))
    rows = exchange(packed, wide_groups)
    turns = STATIONS // 2
    part, up, down = ring_start(mix_sum(targets, mixed), station)
    for s in range(turns - 1):
        part, up, down = ring_turn((part, up, down), s)
    rows, up, down = lax.optimization_barrier((rows, up, down))
    sums = ring_end(ring_turn((part, up, down), turns - 1))

    streams = [ring_start(parts, station) for parts in res_sums(targets, mixed, rows)]
    for s in range(turns):
        streams = [ring_turn(state, s) for state in streams]
    back = [exchange(ring_end(state), wide_groups) for state in streams]

    weight_sum, coadd_flux, both = own_sums(
        exchange(sums.reshape(WIDE, TGT_DEV, -1), wide_groups)
    )
    everything = lax.all_gather(both, "band", axis=2, tiled=True).astype(jnp.float32)
    band_index = lax.axis_index("band")
    shifts = lax.dynamic_slice_in_dim(redshift_shift, band_index * Z_DEV, Z_DEV)
    windows = basis_windows(rest_basis, shifts, 0, everything.shape[2])
    fit_gain = fit_from(*normal_terms(everything[0], everything[1], windows))

    coadd_res = jnp.transpose(finish(weight_sum, back), (1, 0, 2))
    return (coadd_flux, coadd_res, fit_gain)


def solution(mesh):
    in_specs = (P("tgt", "band"), P("tgt", "band"), P("tgt", None, "band"), P(), P(), P(), P())
    out_specs = (P("tgt", "band"), P("tgt", None, "band"), P("tgt", "band"))
    return jax.shard_map(shards, mesh=mesh, in_specs=in_specs, out_specs=out_specs, check_vma=False)
```

```python
import jax
import jax.numpy as jnp
import numpy as np
from jax import lax
from jax.experimental import pallas as pl
from jax.experimental.pallas import tpu as pltpu
from jax.sharding import PartitionSpec as P

TGT_DEV = 16
NDIAG = 11
Z_DEV = 8

XS, ZS, CS = 4, 16, 2
PLANE = XS * CS
QROWS = PLANE * TGT_DEV


def place(x, z, c):
    return ((x % XS) * ZS + z % ZS) * CS + c % CS


plane_groups = [[place(x, z, c) for x in range(XS) for c in range(CS)] for z in range(ZS)]
PAIR = 2
STATIONS = ZS // PAIR
WIDE = PLANE * PAIR
wide_groups = [
    [place(x, h * PAIR + p, c) for x in range(XS) for p in range(PAIR) for c in range(CS)]
    for h in range(STATIONS)
]
ring_groups = [[place(x, z, c) for z in range(ZS)] for x in range(XS) for c in range(CS)]


def ring_step(values, step):
    pairs = [
        (place(x, z, c), place(x, z + step * PAIR, c))
        for x in range(XS)
        for z in range(ZS)
        for c in range(CS)
    ]
    return lax.ppermute(values, "tgt", pairs)


pair_first, pair_second = np.triu_indices(10)


def solve_normal(matrix, right_side):
    basis_count = right_side.shape[0]
    rows_of = [[None] * basis_count for column in range(basis_count)]
    for p in range(len(pair_first)):
        b = int(pair_first[p])
        c = int(pair_second[p])
        rows_of[b][c] = matrix[p]
        rows_of[c][b] = matrix[p]
    vector = [right_side[b] for b in range(basis_count)]
    for k in range(basis_count):
        inverse = 1.0 / rows_of[k][k]
        for r in range(k + 1, basis_count):
            factor = rows_of[r][k] * inverse
            for c in range(k + 1, basis_count):
                rows_of[r][c] = rows_of[r][c] - factor * rows_of[k][c]
            vector[r] = vector[r] - factor * vector[k]
    answer = [None] * basis_count
    for k in reversed(range(basis_count)):
        running = vector[k]
        for c in range(k + 1, basis_count):
            running = running - rows_of[k][c] * answer[c]
        answer[k] = running / rows_of[k][k]
    gain_total = right_side[0] * answer[0]
    for b in range(1, basis_count):
        gain_total = gain_total + right_side[b] * answer[b]
    return gain_total


def basis_windows(rest_basis, shifts, first_wave, length):

    def one_shift(shift_value):
        return lax.dynamic_slice_in_dim(rest_basis, first_wave + shift_value, length, axis=1)

    return jax.vmap(one_shift)(shifts)


def normal_terms(weight_sum, flux_sum, windows):
    products = windows[:, pair_first, :] * windows[:, pair_second, :]
    matrix = jnp.einsum("ti,zpi->ztp", weight_sum, products, precision=lax.Precision.HIGHEST)
    right_side = jnp.einsum("ti,zbi->ztb", flux_sum, windows, precision=lax.Precision.HIGHEST)
    return (matrix, right_side)


def fit_from(matrix, right_side):
    pairs = jnp.transpose(matrix, (2, 0, 1)).reshape(matrix.shape[2], -1)
    sides = jnp.transpose(right_side, (2, 0, 1)).reshape(right_side.shape[2], -1)
    gain = solve_normal(pairs, sides).reshape(matrix.shape[0], matrix.shape[1])
    return gain.T


GROUP = 4


def split_kernel(ivar_ref, res_ref, out_ref):
    lanes = out_ref.shape[-1]
    for part in range(PLANE):
        columns = slice(part * lanes, (part + 1) * lanes)
        out_ref[part, 0] = ivar_ref[:, columns]
        out_ref[part, 1:] = res_ref[:, :, columns]


def split_lanes(ivar, res):
    diagonals, row_count, wave_dev = res.shape
    lanes = wave_dev // PLANE
    return pl.pallas_call(
        split_kernel,
        out_shape=jax.ShapeDtypeStruct((PLANE, diagonals + 1, row_count, lanes), res.dtype),
        compiler_params=pltpu.CompilerParams(vmem_limit_bytes=40 << 20),
        cost_estimate=pl.CostEstimate(
            flops=0, bytes_accessed=4 * (diagonals + 1) * row_count * wave_dev, transcendentals=0
        ),
    )(ivar, res)


def members(target_ref, step):
    per_x = CS * TGT_DEV
    local = lax.broadcasted_iota(jnp.int32, (GROUP * QROWS, 1), 0)
    q = local % QROWS
    plane_z = step * GROUP + local // QROWS
    wanted = (q // per_x) * (ZS * per_x) + plane_z * per_x + q % per_x
    return jnp.where(target_ref[...] == wanted, 1.0, 0.0).astype(jnp.bfloat16)


def res_kernel(target_ref, rows_ref, res_ref, terms):
    sources, planes, row_count, lanes = rows_ref.shape
    step = pl.program_id(0)

    @pl.when(step == 0)
    def fill_terms():
        def one_source(source, carry):
            rows = pl.ds(pl.multiple_of(source * row_count, row_count), row_count)
            weight = rows_ref[source, 0].astype(jnp.float32)
            for plane in range(1, planes):
                product = weight * rows_ref[source, plane].astype(jnp.float32)
                terms[rows, (plane - 1) * lanes : plane * lanes] = product.astype(jnp.bfloat16)
            return carry

        lax.fori_loop(0, sources, one_source, 0)

    sums = jnp.dot(members(target_ref, step), terms[...], preferred_element_type=jnp.float32)
    for g in range(GROUP):
        for owner in range(PLANE):
            first = g * QROWS + owner * TGT_DEV
            block = sums[first : first + TGT_DEV].astype(jnp.bfloat16)
            for diagonal in range(planes - 1):
                res_ref[g, owner, diagonal] = block[:, diagonal * lanes : (diagonal + 1) * lanes]


def coadd_res_rows(targets, rows):
    sources, planes, row_count, lanes = rows.shape
    out_shape = (ZS, PLANE, planes - 1, TGT_DEV, lanes)
    return pl.pallas_call(
        res_kernel,
        out_shape=jax.ShapeDtypeStruct(out_shape, jnp.bfloat16),
        grid=(ZS // GROUP,),
        in_specs=[
            pl.BlockSpec((1, sources * row_count), lambda i: (0, 0)),
            pl.BlockSpec(rows.shape, lambda i: (0, 0, 0, 0)),
        ],
        out_specs=pl.BlockSpec((GROUP,) + out_shape[1:], lambda i: (i, 0, 0, 0, 0)),
        scratch_shapes=[pltpu.VMEM((sources * row_count, (planes - 1) * lanes), jnp.bfloat16)],
        compiler_params=pltpu.CompilerParams(vmem_limit_bytes=56 << 20),
        cost_estimate=pl.CostEstimate(
            flops=2 * ZS * QROWS * sources * row_count * (planes - 1) * lanes,
            bytes_accessed=2 * (rows.size + ZS * QROWS * planes * lanes),
            transcendentals=0,
        ),
    )(targets, rows)


def half_swap(values):
    return pltpu.roll(values, values.shape[-1] // 2, 1)


def mix_kernel(ivar_ref, flux_ref, out_ref):
    row_count, lanes = out_ref.shape[1:]
    first = lax.broadcasted_iota(jnp.int32, (row_count, lanes), 1) < lanes // 2
    for tile in range(WIDE // 2):
        columns = slice(tile * lanes, (tile + 1) * lanes)
        ivar = ivar_ref[:, columns].astype(jnp.float32)
        flux = flux_ref[:, columns].astype(jnp.float32)
        low = jnp.where(first, ivar, half_swap(flux))
        high = jnp.where(first, half_swap(ivar), flux)
        out_ref[2 * tile] = low.astype(out_ref.dtype)
        out_ref[2 * tile + 1] = high.astype(out_ref.dtype)


def mix_pair(ivar, flux):
    row_count, wave_dev = ivar.shape
    return pl.pallas_call(
        mix_kernel,
        out_shape=jax.ShapeDtypeStruct((WIDE, row_count, 2 * wave_dev // WIDE), ivar.dtype),
        cost_estimate=pl.CostEstimate(
            flops=0, bytes_accessed=8 * row_count * wave_dev, transcendentals=0
        ),
    )(ivar, flux)


BATCH = 2


def mix_sum_kernel(target_ref, rows_ref, sums_ref, terms):
    sources, row_count, lanes = rows_ref.shape
    block_rows = WIDE * TGT_DEV
    step = pl.program_id(0)

    @pl.when(step == 0)
    def fill_terms():
        first = lax.broadcasted_iota(jnp.int32, (row_count, lanes), 1) < lanes // 2
        for source in range(sources):
            rows = slice(source * row_count, (source + 1) * row_count)
            values = rows_ref[source].astype(jnp.float32)
            product = jnp.where(first, values, values * half_swap(values))
            rounded = product.astype(jnp.bfloat16)
            terms[rows, 0:lanes] = rounded
            rest = product - rounded.astype(jnp.float32)
            terms[rows, lanes : 2 * lanes] = rest.astype(jnp.bfloat16)

    per_x = PAIR * CS * TGT_DEV
    local = lax.broadcasted_iota(jnp.int32, (BATCH * block_rows, 1), 0)
    q = local % block_rows
    station = step * BATCH + local // block_rows
    wanted = (q // per_x) * (STATIONS * per_x) + station * per_x + q % per_x
    member = jnp.where(target_ref[...] == wanted, 1.0, 0.0).astype(jnp.bfloat16)
    sums = jnp.dot(member, terms[...], preferred_element_type=jnp.float32)
    total = sums[:, 0:lanes] + sums[:, lanes : 2 * lanes]
    for b in range(BATCH):
        sums_ref[b] = total[b * block_rows : (b + 1) * block_rows]


def mix_sum(targets, rows):
    sources, row_count, lanes = rows.shape
    block_rows = WIDE * TGT_DEV
    return pl.pallas_call(
        mix_sum_kernel,
        out_shape=jax.ShapeDtypeStruct((STATIONS, block_rows, lanes), jnp.float32),
        grid=(STATIONS // BATCH,),
        in_specs=[
            pl.BlockSpec((1, sources * row_count), lambda i: (0, 0)),
            pl.BlockSpec(rows.shape, lambda i: (0, 0, 0)),
        ],
        out_specs=pl.BlockSpec((BATCH, block_rows, lanes), lambda i: (i, 0, 0)),
        scratch_shapes=[pltpu.VMEM((sources * row_count, 2 * lanes), jnp.bfloat16)],
        compiler_params=pltpu.CompilerParams(vmem_limit_bytes=40 << 20),
        cost_estimate=pl.CostEstimate(
            flops=4 * STATIONS * block_rows * sources * row_count * lanes,
            bytes_accessed=2 * rows.size + 4 * STATIONS * block_rows * lanes,
            transcendentals=0,
        ),
    )(targets, rows)


def ring_start(parts, station):
    def part(offset):
        return lax.dynamic_index_in_dim(parts, (station + offset) % STATIONS, 0, keepdims=False)

    return part, part(STATIONS // 2), part(STATIONS // 2 + 1)


def ring_turn(state, s):
    half = STATIONS // 2
    part, up, down = state
    up = ring_step(up, 1)
    if s < half - 1:
        up = up + part(half - 1 - s)
        down = ring_step(down, -1)
        if s < half - 2:
            down = down + part(half + 2 + s)
    return part, up, down


def exchange(values, groups):
    return lax.all_to_all(
        values, "tgt", split_axis=0, concat_axis=0, axis_index_groups=groups, tiled=True
    )


def scatter_sum(values):
    return lax.psum_scatter(
        values, "tgt", scatter_dimension=0, axis_index_groups=ring_groups, tiled=False
    )


def shards(
    exposure_flux,
    exposure_ivar,
    exposure_res,
    target_of_row,
    valid_of_row,
    rest_basis,
    redshift_shift,
):
    device = lax.axis_index("tgt")
    my_z = (device // CS) % ZS
    row_count, wave_dev = exposure_flux.shape
    masked = jnp.where(valid_of_row == 1, target_of_row, -1)
    targets = lax.dynamic_index_in_dim(
        masked.reshape(XS, ZS, CS * row_count), my_z, 1, keepdims=False
    ).reshape(1, -1)
    wide_targets = lax.dynamic_index_in_dim(
        masked.reshape(XS, STATIONS, PAIR * CS * row_count), my_z // PAIR, 1, keepdims=False
    ).reshape(1, -1)

    mixed = exchange(mix_pair(exposure_ivar, exposure_flux), wide_groups)
    packed = split_lanes(exposure_ivar, jnp.transpose(exposure_res, (1, 0, 2)))
    packed, mixed = lax.optimization_barrier((packed, mixed))
    rows = exchange(packed, plane_groups)
    turns = STATIONS // 2
    part, up, down = ring_start(mix_sum(wide_targets, mixed), my_z // PAIR)
    for s in range(turns - 1):
        part, up, down = ring_turn((part, up, down), s)
        up, down = lax.optimization_barrier((up, down))
    rows, up, down = lax.optimization_barrier((rows, up, down))
    part, up, down = ring_turn((part, up, down), turns - 1)
    sums = part(0) + up + down
    res_sum = scatter_sum(coadd_res_rows(targets, rows))

    own = exchange(sums.reshape(WIDE, TGT_DEV, -1), wide_groups)
    own = jnp.transpose(own.reshape(WIDE, TGT_DEV, 2, wave_dev // WIDE), (2, 1, 0, 3))
    own = own.reshape(2, TGT_DEV, wave_dev)
    everything = lax.all_gather(own.astype(jnp.bfloat16), "band", axis=2, tiled=True)
    everything = everything.astype(jnp.float32)
    coadd_flux = own[1] / own[0]
    band_index = lax.axis_index("band")
    shifts = lax.dynamic_slice_in_dim(redshift_shift, band_index * Z_DEV, Z_DEV)
    windows = basis_windows(rest_basis, shifts, 0, everything.shape[2])
    fit_gain = fit_from(*normal_terms(everything[0], everything[1], windows))

    back = exchange(res_sum, plane_groups)
    own_res = jnp.transpose(back, (1, 2, 0, 3)).reshape(NDIAG, TGT_DEV, wave_dev)
    coadd_res = (own_res.astype(jnp.float32) / own[0][None]).astype(jnp.bfloat16)
    return (coadd_flux, jnp.transpose(coadd_res, (1, 0, 2)), fit_gain)


def solution(mesh):
    in_specs = (P("tgt", "band"), P("tgt", "band"), P("tgt", None, "band"), P(), P(), P(), P())
    out_specs = (P("tgt", "band"), P("tgt", None, "band"), P("tgt", "band"))
    return jax.shard_map(shards, mesh=mesh, in_specs=in_specs, out_specs=out_specs, check_vma=False)
```

```python
import jax
import jax.numpy as jnp
import numpy as np
from jax import lax
from jax.experimental import pallas as pl
from jax.experimental.pallas import tpu as pltpu
from jax.sharding import PartitionSpec as P

TGT_DEV = 16
NDIAG = 11
Z_DEV = 8

XS, ZS, CS = 4, 16, 2
PLANE = XS * CS
QROWS = PLANE * TGT_DEV


def place(x, z, c):
    return ((x % XS) * ZS + z % ZS) * CS + c % CS


plane_groups = [[place(x, z, c) for x in range(XS) for c in range(CS)] for z in range(ZS)]
PAIR = 2
STATIONS = ZS // PAIR
WIDE = PLANE * PAIR
wide_groups = [
    [place(x, h * PAIR + p, c) for x in range(XS) for p in range(PAIR) for c in range(CS)]
    for h in range(STATIONS)
]
ring_groups = [[place(x, z, c) for z in range(ZS)] for x in range(XS) for c in range(CS)]


def ring_step(values, step):
    pairs = [
        (place(x, z, c), place(x, z + step * PAIR, c))
        for x in range(XS)
        for z in range(ZS)
        for c in range(CS)
    ]
    return lax.ppermute(values, "tgt", pairs)


pair_first, pair_second = np.triu_indices(10)


def solve_normal(matrix, right_side):
    basis_count = right_side.shape[0]
    rows_of = [[None] * basis_count for column in range(basis_count)]
    for p in range(len(pair_first)):
        b = int(pair_first[p])
        c = int(pair_second[p])
        rows_of[b][c] = matrix[p]
        rows_of[c][b] = matrix[p]
    vector = [right_side[b] for b in range(basis_count)]
    for k in range(basis_count):
        inverse = 1.0 / rows_of[k][k]
        for r in range(k + 1, basis_count):
            factor = rows_of[r][k] * inverse
            for c in range(k + 1, basis_count):
                rows_of[r][c] = rows_of[r][c] - factor * rows_of[k][c]
            vector[r] = vector[r] - factor * vector[k]
    answer = [None] * basis_count
    for k in reversed(range(basis_count)):
        running = vector[k]
        for c in range(k + 1, basis_count):
            running = running - rows_of[k][c] * answer[c]
        answer[k] = running / rows_of[k][k]
    gain_total = right_side[0] * answer[0]
    for b in range(1, basis_count):
        gain_total = gain_total + right_side[b] * answer[b]
    return gain_total


def basis_windows(rest_basis, shifts, first_wave, length):

    def one_shift(shift_value):
        return lax.dynamic_slice_in_dim(rest_basis, first_wave + shift_value, length, axis=1)

    return jax.vmap(one_shift)(shifts)


def normal_terms(weight_sum, flux_sum, windows):
    products = windows[:, pair_first, :] * windows[:, pair_second, :]
    matrix = jnp.einsum("ti,zpi->ztp", weight_sum, products, precision=lax.Precision.HIGHEST)
    right_side = jnp.einsum("ti,zbi->ztb", flux_sum, windows, precision=lax.Precision.HIGHEST)
    return (matrix, right_side)


def fit_from(matrix, right_side):
    pairs = jnp.transpose(matrix, (2, 0, 1)).reshape(matrix.shape[2], -1)
    sides = jnp.transpose(right_side, (2, 0, 1)).reshape(right_side.shape[2], -1)
    gain = solve_normal(pairs, sides).reshape(matrix.shape[0], matrix.shape[1])
    return gain.T


GROUP = 4


def split_kernel(ivar_ref, res_ref, out_ref):
    lanes = out_ref.shape[-1]
    for part in range(PLANE):
        columns = slice(part * lanes, (part + 1) * lanes)
        out_ref[part, 0] = ivar_ref[:, columns]
        out_ref[part, 1:] = res_ref[:, :, columns]


def split_lanes(ivar, res):
    diagonals, row_count, wave_dev = res.shape
    lanes = wave_dev // PLANE
    return pl.pallas_call(
        split_kernel,
        out_shape=jax.ShapeDtypeStruct((PLANE, diagonals + 1, row_count, lanes), res.dtype),
        compiler_params=pltpu.CompilerParams(vmem_limit_bytes=40 << 20),
        cost_estimate=pl.CostEstimate(
            flops=0, bytes_accessed=4 * (diagonals + 1) * row_count * wave_dev, transcendentals=0
        ),
    )(ivar, res)


def members(target_ref, step):
    per_x = CS * TGT_DEV
    local = lax.broadcasted_iota(jnp.int32, (GROUP * QROWS, 1), 0)
    q = local % QROWS
    plane_z = step * GROUP + local // QROWS
    wanted = (q // per_x) * (ZS * per_x) + plane_z * per_x + q % per_x
    return jnp.where(target_ref[...] == wanted, 1.0, 0.0).astype(jnp.bfloat16)


def res_kernel(target_ref, rows_ref, res_ref, terms):
    sources, planes, row_count, lanes = rows_ref.shape
    step = pl.program_id(0)

    @pl.when(step == 0)
    def fill_terms():
        def one_source(source, carry):
            rows = pl.ds(pl.multiple_of(source * row_count, row_count), row_count)
            weight = rows_ref[source, 0]
            for plane in range(1, planes):
                product = weight * rows_ref[source, plane]
                terms[rows, (plane - 1) * lanes : plane * lanes] = product
            return carry

        lax.fori_loop(0, sources, one_source, 0)

    sums = jnp.dot(members(target_ref, step), terms[...], preferred_element_type=jnp.float32)
    for g in range(GROUP):
        for owner in range(PLANE):
            first = g * QROWS + owner * TGT_DEV
            block = sums[first : first + TGT_DEV].astype(jnp.bfloat16)
            for diagonal in range(planes - 1):
                res_ref[g, owner, diagonal] = block[:, diagonal * lanes : (diagonal + 1) * lanes]


def coadd_res_rows(targets, rows):
    sources, planes, row_count, lanes = rows.shape
    out_shape = (ZS, PLANE, planes - 1, TGT_DEV, lanes)
    return pl.pallas_call(
        res_kernel,
        out_shape=jax.ShapeDtypeStruct(out_shape, jnp.bfloat16),
        grid=(ZS // GROUP,),
        in_specs=[
            pl.BlockSpec((1, sources * row_count), lambda i: (0, 0)),
            pl.BlockSpec(rows.shape, lambda i: (0, 0, 0, 0)),
        ],
        out_specs=pl.BlockSpec((GROUP,) + out_shape[1:], lambda i: (i, 0, 0, 0, 0)),
        scratch_shapes=[pltpu.VMEM((sources * row_count, (planes - 1) * lanes), jnp.bfloat16)],
        compiler_params=pltpu.CompilerParams(vmem_limit_bytes=56 << 20),
        cost_estimate=pl.CostEstimate(
            flops=2 * ZS * QROWS * sources * row_count * (planes - 1) * lanes,
            bytes_accessed=2 * (rows.size + ZS * QROWS * planes * lanes),
            transcendentals=0,
        ),
    )(targets, rows)


def half_swap(values):
    return pltpu.roll(values, values.shape[-1] // 2, 1)


def mix_kernel(ivar_ref, flux_ref, out_ref):
    row_count, lanes = out_ref.shape[1:]
    first = lax.broadcasted_iota(jnp.int32, (row_count, lanes), 1) < lanes // 2
    for tile in range(WIDE // 2):
        columns = slice(tile * lanes, (tile + 1) * lanes)
        ivar = ivar_ref[:, columns].astype(jnp.float32)
        flux = flux_ref[:, columns].astype(jnp.float32)
        low = jnp.where(first, ivar, half_swap(flux))
        high = jnp.where(first, half_swap(ivar), flux)
        out_ref[2 * tile] = low.astype(out_ref.dtype)
        out_ref[2 * tile + 1] = high.astype(out_ref.dtype)


def mix_pair(ivar, flux):
    row_count, wave_dev = ivar.shape
    return pl.pallas_call(
        mix_kernel,
        out_shape=jax.ShapeDtypeStruct((WIDE, row_count, 2 * wave_dev // WIDE), ivar.dtype),
        cost_estimate=pl.CostEstimate(
            flops=0, bytes_accessed=8 * row_count * wave_dev, transcendentals=0
        ),
    )(ivar, flux)


BATCH = 2


def mix_sum_kernel(target_ref, rows_ref, sums_ref, terms):
    sources, row_count, lanes = rows_ref.shape
    block_rows = WIDE * TGT_DEV
    step = pl.program_id(0)

    @pl.when(step == 0)
    def fill_terms():
        first = lax.broadcasted_iota(jnp.int32, (row_count, lanes), 1) < lanes // 2
        for source in range(sources):
            rows = slice(source * row_count, (source + 1) * row_count)
            values = rows_ref[source].astype(jnp.float32)
            product = jnp.where(first, values, values * half_swap(values))
            rounded = product.astype(jnp.bfloat16)
            terms[rows, 0:lanes] = rounded
            rest = product - rounded.astype(jnp.float32)
            terms[rows, lanes : 2 * lanes] = rest.astype(jnp.bfloat16)

    per_x = PAIR * CS * TGT_DEV
    local = lax.broadcasted_iota(jnp.int32, (BATCH * block_rows, 1), 0)
    q = local % block_rows
    station = step * BATCH + local // block_rows
    wanted = (q // per_x) * (STATIONS * per_x) + station * per_x + q % per_x
    member = jnp.where(target_ref[...] == wanted, 1.0, 0.0).astype(jnp.bfloat16)
    sums = jnp.dot(member, terms[...], preferred_element_type=jnp.float32)
    total = sums[:, 0:lanes] + sums[:, lanes : 2 * lanes]
    for b in range(BATCH):
        sums_ref[b] = total[b * block_rows : (b + 1) * block_rows]


def mix_sum(targets, rows):
    sources, row_count, lanes = rows.shape
    block_rows = WIDE * TGT_DEV
    return pl.pallas_call(
        mix_sum_kernel,
        out_shape=jax.ShapeDtypeStruct((STATIONS, block_rows, lanes), jnp.float32),
        grid=(STATIONS // BATCH,),
        in_specs=[
            pl.BlockSpec((1, sources * row_count), lambda i: (0, 0)),
            pl.BlockSpec(rows.shape, lambda i: (0, 0, 0)),
        ],
        out_specs=pl.BlockSpec((BATCH, block_rows, lanes), lambda i: (i, 0, 0)),
        scratch_shapes=[pltpu.VMEM((sources * row_count, 2 * lanes), jnp.bfloat16)],
        compiler_params=pltpu.CompilerParams(vmem_limit_bytes=40 << 20),
        cost_estimate=pl.CostEstimate(
            flops=4 * STATIONS * block_rows * sources * row_count * lanes,
            bytes_accessed=2 * rows.size + 4 * STATIONS * block_rows * lanes,
            transcendentals=0,
        ),
    )(targets, rows)


def ring_start(parts, station):
    def part(offset):
        return lax.dynamic_index_in_dim(parts, (station + offset) % STATIONS, 0, keepdims=False)

    return part, part(STATIONS // 2), part(STATIONS // 2 + 1)


def ring_turn(state, s):
    half = STATIONS // 2
    part, up, down = state
    up = ring_step(up, 1)
    if s < half - 1:
        up = up + part(half - 1 - s)
        down = ring_step(down, -1)
        if s < half - 2:
            down = down + part(half + 2 + s)
    return part, up, down


def exchange(values, groups):
    return lax.all_to_all(
        values, "tgt", split_axis=0, concat_axis=0, axis_index_groups=groups, tiled=True
    )


def scatter_sum(values):
    return lax.psum_scatter(
        values, "tgt", scatter_dimension=0, axis_index_groups=ring_groups, tiled=False
    )


def shards(
    exposure_flux,
    exposure_ivar,
    exposure_res,
    target_of_row,
    valid_of_row,
    rest_basis,
    redshift_shift,
):
    device = lax.axis_index("tgt")
    my_z = (device // CS) % ZS
    row_count, wave_dev = exposure_flux.shape
    masked = jnp.where(valid_of_row == 1, target_of_row, -1)
    targets = lax.dynamic_index_in_dim(
        masked.reshape(XS, ZS, CS * row_count), my_z, 1, keepdims=False
    ).reshape(1, -1)
    wide_targets = lax.dynamic_index_in_dim(
        masked.reshape(XS, STATIONS, PAIR * CS * row_count), my_z // PAIR, 1, keepdims=False
    ).reshape(1, -1)

    mixed = exchange(mix_pair(exposure_ivar, exposure_flux), wide_groups)
    packed = split_lanes(exposure_ivar, jnp.transpose(exposure_res, (1, 0, 2)))
    packed, mixed = lax.optimization_barrier((packed, mixed))
    rows = exchange(packed, plane_groups)
    turns = STATIONS // 2
    part, up, down = ring_start(mix_sum(wide_targets, mixed), my_z // PAIR)
    for s in range(turns):
        if s == turns // 2:
            rows, up, down = lax.optimization_barrier((rows, up, down))
        part, up, down = ring_turn((part, up, down), s)
        if s < turns - 1:
            up, down = lax.optimization_barrier((up, down))
    sums = part(0) + up + down
    res_sum = scatter_sum(coadd_res_rows(targets, rows))

    own = exchange(sums.reshape(WIDE, TGT_DEV, -1), wide_groups)
    own = jnp.transpose(own.reshape(WIDE, TGT_DEV, 2, wave_dev // WIDE), (2, 1, 0, 3))
    own = own.reshape(2, TGT_DEV, wave_dev)
    everything = lax.all_gather(own.astype(jnp.bfloat16), "band", axis=2, tiled=True)
    everything = everything.astype(jnp.float32)
    coadd_flux = own[1] / own[0]
    band_index = lax.axis_index("band")
    shifts = lax.dynamic_slice_in_dim(redshift_shift, band_index * Z_DEV, Z_DEV)
    windows = basis_windows(rest_basis, shifts, 0, everything.shape[2])
    fit_gain = fit_from(*normal_terms(everything[0], everything[1], windows))

    back = exchange(res_sum, plane_groups)
    own_res = jnp.transpose(back, (1, 2, 0, 3)).reshape(NDIAG, TGT_DEV, wave_dev)
    coadd_res = (own_res.astype(jnp.float32) / own[0][None]).astype(jnp.bfloat16)
    return (coadd_flux, jnp.transpose(coadd_res, (1, 0, 2)), fit_gain)


def solution(mesh):
    in_specs = (P("tgt", "band"), P("tgt", "band"), P("tgt", None, "band"), P(), P(), P(), P())
    out_specs = (P("tgt", "band"), P("tgt", None, "band"), P("tgt", "band"))
    return jax.shard_map(shards, mesh=mesh, in_specs=in_specs, out_specs=out_specs, check_vma=False)
```

```python
import jax
import jax.numpy as jnp
import numpy as np
from jax import lax
from jax.experimental import pallas as pl
from jax.experimental.pallas import tpu as pltpu
from jax.sharding import PartitionSpec as P

TGT_DEV = 16
NDIAG = 11
Z_DEV = 8

XS, ZS, CS = 4, 16, 2
PLANE = XS * CS
QROWS = PLANE * TGT_DEV


def place(x, z, c):
    return ((x % XS) * ZS + z % ZS) * CS + c % CS


plane_groups = [[place(x, z, c) for x in range(XS) for c in range(CS)] for z in range(ZS)]
PAIR = 2
STATIONS = ZS // PAIR
WIDE = PLANE * PAIR
wide_groups = [
    [place(x, h * PAIR + p, c) for x in range(XS) for p in range(PAIR) for c in range(CS)]
    for h in range(STATIONS)
]
ring_groups = [[place(x, z, c) for z in range(ZS)] for x in range(XS) for c in range(CS)]


def ring_step(values, step):
    pairs = [
        (place(x, z, c), place(x, z + step * PAIR, c))
        for x in range(XS)
        for z in range(ZS)
        for c in range(CS)
    ]
    return lax.ppermute(values, "tgt", pairs)


pair_first, pair_second = np.triu_indices(10)


def solve_normal(matrix, right_side):
    basis_count = right_side.shape[0]
    rows_of = [[None] * basis_count for column in range(basis_count)]
    for p in range(len(pair_first)):
        b = int(pair_first[p])
        c = int(pair_second[p])
        rows_of[b][c] = matrix[p]
        rows_of[c][b] = matrix[p]
    vector = [right_side[b] for b in range(basis_count)]
    for k in range(basis_count):
        inverse = 1.0 / rows_of[k][k]
        for r in range(k + 1, basis_count):
            factor = rows_of[r][k] * inverse
            for c in range(k + 1, basis_count):
                rows_of[r][c] = rows_of[r][c] - factor * rows_of[k][c]
            vector[r] = vector[r] - factor * vector[k]
    answer = [None] * basis_count
    for k in reversed(range(basis_count)):
        running = vector[k]
        for c in range(k + 1, basis_count):
            running = running - rows_of[k][c] * answer[c]
        answer[k] = running / rows_of[k][k]
    gain_total = right_side[0] * answer[0]
    for b in range(1, basis_count):
        gain_total = gain_total + right_side[b] * answer[b]
    return gain_total


def basis_windows(rest_basis, shifts, first_wave, length):

    def one_shift(shift_value):
        return lax.dynamic_slice_in_dim(rest_basis, first_wave + shift_value, length, axis=1)

    return jax.vmap(one_shift)(shifts)


def normal_terms(weight_sum, flux_sum, windows):
    products = windows[:, pair_first, :] * windows[:, pair_second, :]
    matrix = jnp.einsum("ti,zpi->ztp", weight_sum, products, precision=lax.Precision.HIGHEST)
    right_side = jnp.einsum("ti,zbi->ztb", flux_sum, windows, precision=lax.Precision.HIGHEST)
    return (matrix, right_side)


def fit_from(matrix, right_side):
    pairs = jnp.transpose(matrix, (2, 0, 1)).reshape(matrix.shape[2], -1)
    sides = jnp.transpose(right_side, (2, 0, 1)).reshape(right_side.shape[2], -1)
    gain = solve_normal(pairs, sides).reshape(matrix.shape[0], matrix.shape[1])
    return gain.T


GROUP = 4


def split_kernel(ivar_ref, res_ref, out_ref):
    lanes = out_ref.shape[-1]
    for part in range(PLANE):
        columns = slice(part * lanes, (part + 1) * lanes)
        weight = ivar_ref[:, columns]
        for diagonal in range(NDIAG):
            out_ref[part, diagonal] = weight * res_ref[diagonal, :, columns]


def split_lanes(ivar, res):
    diagonals, row_count, wave_dev = res.shape
    lanes = wave_dev // PLANE
    return pl.pallas_call(
        split_kernel,
        out_shape=jax.ShapeDtypeStruct((PLANE, diagonals, row_count, lanes), res.dtype),
        compiler_params=pltpu.CompilerParams(vmem_limit_bytes=40 << 20),
        cost_estimate=pl.CostEstimate(
            flops=diagonals * row_count * wave_dev,
            bytes_accessed=4 * (diagonals + 1) * row_count * wave_dev,
            transcendentals=0,
        ),
    )(ivar, res)


def members(target_ref, step):
    per_x = CS * TGT_DEV
    local = lax.broadcasted_iota(jnp.int32, (GROUP * QROWS, 1), 0)
    q = local % QROWS
    plane_z = step * GROUP + local // QROWS
    wanted = (q // per_x) * (ZS * per_x) + plane_z * per_x + q % per_x
    return jnp.where(target_ref[...] == wanted, 1.0, 0.0).astype(jnp.bfloat16)


def res_kernel(target_ref, rows_ref, res_ref, terms):
    sources, planes, row_count, lanes = rows_ref.shape
    step = pl.program_id(0)

    @pl.when(step == 0)
    def fill_terms():
        def one_source(source, carry):
            rows = pl.ds(pl.multiple_of(source * row_count, row_count), row_count)
            for plane in range(planes):
                terms[rows, plane * lanes : (plane + 1) * lanes] = rows_ref[source, plane]
            return carry

        lax.fori_loop(0, sources, one_source, 0)

    sums = jnp.dot(members(target_ref, step), terms[...], preferred_element_type=jnp.float32)
    for g in range(GROUP):
        for owner in range(PLANE):
            first = g * QROWS + owner * TGT_DEV
            block = sums[first : first + TGT_DEV].astype(jnp.bfloat16)
            for diagonal in range(planes):
                res_ref[g, owner, diagonal] = block[:, diagonal * lanes : (diagonal + 1) * lanes]


def coadd_res_rows(targets, rows):
    sources, planes, row_count, lanes = rows.shape
    out_shape = (ZS, PLANE, planes, TGT_DEV, lanes)
    return pl.pallas_call(
        res_kernel,
        out_shape=jax.ShapeDtypeStruct(out_shape, jnp.bfloat16),
        grid=(ZS // GROUP,),
        in_specs=[
            pl.BlockSpec((1, sources * row_count), lambda i: (0, 0)),
            pl.BlockSpec(rows.shape, lambda i: (0, 0, 0, 0)),
        ],
        out_specs=pl.BlockSpec((GROUP,) + out_shape[1:], lambda i: (i, 0, 0, 0, 0)),
        scratch_shapes=[pltpu.VMEM((sources * row_count, planes * lanes), jnp.bfloat16)],
        compiler_params=pltpu.CompilerParams(vmem_limit_bytes=56 << 20),
        cost_estimate=pl.CostEstimate(
            flops=2 * ZS * QROWS * sources * row_count * planes * lanes,
            bytes_accessed=2 * (rows.size + ZS * QROWS * planes * lanes),
            transcendentals=0,
        ),
    )(targets, rows)


def half_swap(values):
    return pltpu.roll(values, values.shape[-1] // 2, 1)


def mix_kernel(ivar_ref, flux_ref, out_ref):
    row_count, lanes = out_ref.shape[1:]
    first = lax.broadcasted_iota(jnp.int32, (row_count, lanes), 1) < lanes // 2
    for tile in range(WIDE // 2):
        columns = slice(tile * lanes, (tile + 1) * lanes)
        ivar = ivar_ref[:, columns].astype(jnp.float32)
        flux = flux_ref[:, columns].astype(jnp.float32)
        low = jnp.where(first, ivar, half_swap(flux))
        high = jnp.where(first, half_swap(ivar), flux)
        out_ref[2 * tile] = low.astype(out_ref.dtype)
        out_ref[2 * tile + 1] = high.astype(out_ref.dtype)


def mix_pair(ivar, flux):
    row_count, wave_dev = ivar.shape
    return pl.pallas_call(
        mix_kernel,
        out_shape=jax.ShapeDtypeStruct((WIDE, row_count, 2 * wave_dev // WIDE), ivar.dtype),
        cost_estimate=pl.CostEstimate(
            flops=0, bytes_accessed=8 * row_count * wave_dev, transcendentals=0
        ),
    )(ivar, flux)


BATCH = 2


def mix_sum_kernel(target_ref, rows_ref, sums_ref, terms):
    sources, row_count, lanes = rows_ref.shape
    block_rows = WIDE * TGT_DEV
    step = pl.program_id(0)

    @pl.when(step == 0)
    def fill_terms():
        first = lax.broadcasted_iota(jnp.int32, (row_count, lanes), 1) < lanes // 2
        for source in range(sources):
            rows = slice(source * row_count, (source + 1) * row_count)
            values = rows_ref[source].astype(jnp.float32)
            product = jnp.where(first, values, values * half_swap(values))
            rounded = product.astype(jnp.bfloat16)
            terms[rows, 0:lanes] = rounded
            rest = product - rounded.astype(jnp.float32)
            terms[rows, lanes : 2 * lanes] = rest.astype(jnp.bfloat16)

    per_x = PAIR * CS * TGT_DEV
    local = lax.broadcasted_iota(jnp.int32, (BATCH * block_rows, 1), 0)
    q = local % block_rows
    station = step * BATCH + local // block_rows
    wanted = (q // per_x) * (STATIONS * per_x) + station * per_x + q % per_x
    member = jnp.where(target_ref[...] == wanted, 1.0, 0.0).astype(jnp.bfloat16)
    sums = jnp.dot(member, terms[...], preferred_element_type=jnp.float32)
    total = sums[:, 0:lanes] + sums[:, lanes : 2 * lanes]
    for b in range(BATCH):
        sums_ref[b] = total[b * block_rows : (b + 1) * block_rows]


def mix_sum(targets, rows):
    sources, row_count, lanes = rows.shape
    block_rows = WIDE * TGT_DEV
    return pl.pallas_call(
        mix_sum_kernel,
        out_shape=jax.ShapeDtypeStruct((STATIONS, block_rows, lanes), jnp.float32),
        grid=(STATIONS // BATCH,),
        in_specs=[
            pl.BlockSpec((1, sources * row_count), lambda i: (0, 0)),
            pl.BlockSpec(rows.shape, lambda i: (0, 0, 0)),
        ],
        out_specs=pl.BlockSpec((BATCH, block_rows, lanes), lambda i: (i, 0, 0)),
        scratch_shapes=[pltpu.VMEM((sources * row_count, 2 * lanes), jnp.bfloat16)],
        compiler_params=pltpu.CompilerParams(vmem_limit_bytes=40 << 20),
        cost_estimate=pl.CostEstimate(
            flops=4 * STATIONS * block_rows * sources * row_count * lanes,
            bytes_accessed=2 * rows.size + 4 * STATIONS * block_rows * lanes,
            transcendentals=0,
        ),
    )(targets, rows)


def ring_start(parts, station):
    def part(offset):
        return lax.dynamic_index_in_dim(parts, (station + offset) % STATIONS, 0, keepdims=False)

    return part, part(STATIONS // 2), part(STATIONS // 2 + 1)


def ring_turn(state, s):
    half = STATIONS // 2
    part, up, down = state
    up = ring_step(up, 1)
    if s < half - 1:
        up = up + part(half - 1 - s)
        down = ring_step(down, -1)
        if s < half - 2:
            down = down + part(half + 2 + s)
    return part, up, down


def exchange(values, groups):
    return lax.all_to_all(
        values, "tgt", split_axis=0, concat_axis=0, axis_index_groups=groups, tiled=True
    )


def scatter_sum(values):
    return lax.psum_scatter(
        values, "tgt", scatter_dimension=0, axis_index_groups=ring_groups, tiled=False
    )


def shards(
    exposure_flux,
    exposure_ivar,
    exposure_res,
    target_of_row,
    valid_of_row,
    rest_basis,
    redshift_shift,
):
    device = lax.axis_index("tgt")
    my_z = (device // CS) % ZS
    row_count, wave_dev = exposure_flux.shape
    masked = jnp.where(valid_of_row == 1, target_of_row, -1)
    targets = lax.dynamic_index_in_dim(
        masked.reshape(XS, ZS, CS * row_count), my_z, 1, keepdims=False
    ).reshape(1, -1)
    wide_targets = lax.dynamic_index_in_dim(
        masked.reshape(XS, STATIONS, PAIR * CS * row_count), my_z // PAIR, 1, keepdims=False
    ).reshape(1, -1)

    mixed = exchange(mix_pair(exposure_ivar, exposure_flux), wide_groups)
    packed = split_lanes(exposure_ivar, jnp.transpose(exposure_res, (1, 0, 2)))
    packed, mixed = lax.optimization_barrier((packed, mixed))
    rows = exchange(packed, plane_groups)
    turns = STATIONS // 2
    part, up, down = ring_start(mix_sum(wide_targets, mixed), my_z // PAIR)
    for s in range(turns):
        if s == turns // 2:
            rows, up, down = lax.optimization_barrier((rows, up, down))
        part, up, down = ring_turn((part, up, down), s)
        if s < turns - 1:
            up, down = lax.optimization_barrier((up, down))
    sums = part(0) + up + down
    res_sum = scatter_sum(coadd_res_rows(targets, rows))

    own = exchange(sums.reshape(WIDE, TGT_DEV, -1), wide_groups)
    own = jnp.transpose(own.reshape(WIDE, TGT_DEV, 2, wave_dev // WIDE), (2, 1, 0, 3))
    own = own.reshape(2, TGT_DEV, wave_dev)
    everything = lax.all_gather(own.astype(jnp.bfloat16), "band", axis=2, tiled=True)
    everything = everything.astype(jnp.float32)
    coadd_flux = own[1] / own[0]
    band_index = lax.axis_index("band")
    shifts = lax.dynamic_slice_in_dim(redshift_shift, band_index * Z_DEV, Z_DEV)
    windows = basis_windows(rest_basis, shifts, 0, everything.shape[2])
    fit_gain = fit_from(*normal_terms(everything[0], everything[1], windows))

    back = exchange(res_sum, plane_groups)
    own_res = jnp.transpose(back, (1, 2, 0, 3)).reshape(NDIAG, TGT_DEV, wave_dev)
    coadd_res = (own_res.astype(jnp.float32) / own[0][None]).astype(jnp.bfloat16)
    return (coadd_flux, jnp.transpose(coadd_res, (1, 0, 2)), fit_gain)


def solution(mesh):
    in_specs = (P("tgt", "band"), P("tgt", "band"), P("tgt", None, "band"), P(), P(), P(), P())
    out_specs = (P("tgt", "band"), P("tgt", None, "band"), P("tgt", "band"))
    return jax.shard_map(shards, mesh=mesh, in_specs=in_specs, out_specs=out_specs, check_vma=False)
```

```python
import jax
import jax.numpy as jnp
import numpy as np
from jax import lax
from jax.experimental import pallas as pl
from jax.experimental.pallas import tpu as pltpu
from jax.sharding import PartitionSpec as P

TGT_DEV = 16
NDIAG = 11
Z_DEV = 8
SHIFT = 512

XS, ZS, CS = 4, 16, 2
PLANE = XS * CS
QROWS = PLANE * TGT_DEV


def place(x, z, c):
    return ((x % XS) * ZS + z % ZS) * CS + c % CS


plane_groups = [[place(x, z, c) for x in range(XS) for c in range(CS)] for z in range(ZS)]
PAIR = 2
STATIONS = ZS // PAIR
WIDE = PLANE * PAIR
wide_groups = [
    [place(x, h * PAIR + p, c) for x in range(XS) for p in range(PAIR) for c in range(CS)]
    for h in range(STATIONS)
]
ring_groups = [[place(x, z, c) for z in range(ZS)] for x in range(XS) for c in range(CS)]


def ring_step(values, step):
    pairs = [
        (place(x, z, c), place(x, z + step * PAIR, c))
        for x in range(XS)
        for z in range(ZS)
        for c in range(CS)
    ]
    return lax.ppermute(values, "tgt", pairs)


pair_first, pair_second = np.triu_indices(10)


def solve_normal(matrix, right_side):
    basis_count = right_side.shape[0]
    rows_of = [[None] * basis_count for column in range(basis_count)]
    for p in range(len(pair_first)):
        b = int(pair_first[p])
        c = int(pair_second[p])
        rows_of[b][c] = matrix[p]
        rows_of[c][b] = matrix[p]
    vector = [right_side[b] for b in range(basis_count)]
    for k in range(basis_count):
        inverse = 1.0 / rows_of[k][k]
        for r in range(k + 1, basis_count):
            factor = rows_of[r][k] * inverse
            for c in range(k + 1, basis_count):
                rows_of[r][c] = rows_of[r][c] - factor * rows_of[k][c]
            vector[r] = vector[r] - factor * vector[k]
    answer = [None] * basis_count
    for k in reversed(range(basis_count)):
        running = vector[k]
        for c in range(k + 1, basis_count):
            running = running - rows_of[k][c] * answer[c]
        answer[k] = running / rows_of[k][k]
    gain_total = right_side[0] * answer[0]
    for b in range(1, basis_count):
        gain_total = gain_total + right_side[b] * answer[b]
    return gain_total


def basis_windows(rest_basis, shifts, first_wave, length):

    def one_shift(shift_value):
        return lax.dynamic_slice_in_dim(rest_basis, first_wave + shift_value, length, axis=1)

    return jax.vmap(one_shift)(shifts)


def normal_terms(weight_sum, flux_sum, windows, firsts, seconds):
    products = firsts * seconds
    matrix = jnp.einsum("ti,zpi->ztp", weight_sum, products, precision=lax.Precision.HIGHEST)
    right_side = jnp.einsum("ti,zbi->ztb", flux_sum, windows, precision=lax.Precision.HIGHEST)
    return (matrix, right_side)


def fit_from(matrix, right_side):
    pairs = jnp.transpose(matrix, (2, 0, 1)).reshape(matrix.shape[2], -1)
    sides = jnp.transpose(right_side, (2, 0, 1)).reshape(right_side.shape[2], -1)
    gain = solve_normal(pairs, sides).reshape(matrix.shape[0], matrix.shape[1])
    return gain.T


GROUP = 4


def split_kernel(ivar_ref, res_ref, out_ref):
    lanes = out_ref.shape[-1]
    for part in range(PLANE):
        columns = slice(part * lanes, (part + 1) * lanes)
        weight = ivar_ref[:, columns]
        for diagonal in range(NDIAG):
            out_ref[part, diagonal] = weight * res_ref[diagonal, :, columns]


def split_lanes(ivar, res):
    diagonals, row_count, wave_dev = res.shape
    lanes = wave_dev // PLANE
    return pl.pallas_call(
        split_kernel,
        out_shape=jax.ShapeDtypeStruct((PLANE, diagonals, row_count, lanes), res.dtype),
        compiler_params=pltpu.CompilerParams(vmem_limit_bytes=40 << 20),
        cost_estimate=pl.CostEstimate(
            flops=diagonals * row_count * wave_dev,
            bytes_accessed=4 * (diagonals + 1) * row_count * wave_dev,
            transcendentals=0,
        ),
    )(ivar, res)


def members(target_ref, step):
    per_x = CS * TGT_DEV
    local = lax.broadcasted_iota(jnp.int32, (GROUP * QROWS, 1), 0)
    q = local % QROWS
    plane_z = step * GROUP + local // QROWS
    wanted = (q // per_x) * (ZS * per_x) + plane_z * per_x + q % per_x
    return jnp.where(target_ref[...] == wanted, 1.0, 0.0).astype(jnp.bfloat16)


def res_kernel(target_ref, rows_ref, res_ref, terms):
    sources, planes, row_count, lanes = rows_ref.shape
    step = pl.program_id(0)

    @pl.when(step == 0)
    def fill_terms():
        def one_source(source, carry):
            rows = pl.ds(pl.multiple_of(source * row_count, row_count), row_count)
            for plane in range(planes):
                terms[rows, plane * lanes : (plane + 1) * lanes] = rows_ref[source, plane]
            return carry

        lax.fori_loop(0, sources, one_source, 0)

    sums = jnp.dot(members(target_ref, step), terms[...], preferred_element_type=jnp.float32)
    for g in range(GROUP):
        for owner in range(PLANE):
            first = g * QROWS + owner * TGT_DEV
            block = sums[first : first + TGT_DEV].astype(jnp.bfloat16)
            for diagonal in range(planes):
                res_ref[g, owner, diagonal] = block[:, diagonal * lanes : (diagonal + 1) * lanes]


def coadd_res_rows(targets, rows):
    sources, planes, row_count, lanes = rows.shape
    out_shape = (ZS, PLANE, planes, TGT_DEV, lanes)
    return pl.pallas_call(
        res_kernel,
        out_shape=jax.ShapeDtypeStruct(out_shape, jnp.bfloat16),
        grid=(ZS // GROUP,),
        in_specs=[
            pl.BlockSpec((1, sources * row_count), lambda i: (0, 0)),
            pl.BlockSpec(rows.shape, lambda i: (0, 0, 0, 0)),
        ],
        out_specs=pl.BlockSpec((GROUP,) + out_shape[1:], lambda i: (i, 0, 0, 0, 0)),
        scratch_shapes=[pltpu.VMEM((sources * row_count, planes * lanes), jnp.bfloat16)],
        compiler_params=pltpu.CompilerParams(vmem_limit_bytes=56 << 20),
        cost_estimate=pl.CostEstimate(
            flops=2 * ZS * QROWS * sources * row_count * planes * lanes,
            bytes_accessed=2 * (rows.size + ZS * QROWS * planes * lanes),
            transcendentals=0,
        ),
    )(targets, rows)


def half_swap(values):
    return pltpu.roll(values, values.shape[-1] // 2, 1)


def mix_kernel(ivar_ref, flux_ref, out_ref):
    row_count, lanes = out_ref.shape[1:]
    first = lax.broadcasted_iota(jnp.int32, (row_count, lanes), 1) < lanes // 2
    for tile in range(WIDE // 2):
        columns = slice(tile * lanes, (tile + 1) * lanes)
        ivar = ivar_ref[:, columns].astype(jnp.float32)
        flux = flux_ref[:, columns].astype(jnp.float32)
        low = jnp.where(first, ivar, half_swap(flux))
        high = jnp.where(first, half_swap(ivar), flux)
        out_ref[2 * tile] = low.astype(out_ref.dtype)
        out_ref[2 * tile + 1] = high.astype(out_ref.dtype)


def mix_pair(ivar, flux):
    row_count, wave_dev = ivar.shape
    return pl.pallas_call(
        mix_kernel,
        out_shape=jax.ShapeDtypeStruct((WIDE, row_count, 2 * wave_dev // WIDE), ivar.dtype),
        cost_estimate=pl.CostEstimate(
            flops=0, bytes_accessed=8 * row_count * wave_dev, transcendentals=0
        ),
    )(ivar, flux)


BATCH = 2


def mix_sum_kernel(target_ref, rows_ref, sums_ref, terms):
    sources, row_count, lanes = rows_ref.shape
    block_rows = WIDE * TGT_DEV
    step = pl.program_id(0)

    @pl.when(step == 0)
    def fill_terms():
        first = lax.broadcasted_iota(jnp.int32, (row_count, lanes), 1) < lanes // 2
        for source in range(sources):
            rows = slice(source * row_count, (source + 1) * row_count)
            values = rows_ref[source].astype(jnp.float32)
            product = jnp.where(first, values, values * half_swap(values))
            rounded = product.astype(jnp.bfloat16)
            terms[rows, 0:lanes] = rounded
            rest = product - rounded.astype(jnp.float32)
            terms[rows, lanes : 2 * lanes] = rest.astype(jnp.bfloat16)

    per_x = PAIR * CS * TGT_DEV
    local = lax.broadcasted_iota(jnp.int32, (BATCH * block_rows, 1), 0)
    q = local % block_rows
    station = step * BATCH + local // block_rows
    wanted = (q // per_x) * (STATIONS * per_x) + station * per_x + q % per_x
    member = jnp.where(target_ref[...] == wanted, 1.0, 0.0).astype(jnp.bfloat16)
    sums = jnp.dot(member, terms[...], preferred_element_type=jnp.float32)
    total = sums[:, 0:lanes] + sums[:, lanes : 2 * lanes]
    for b in range(BATCH):
        sums_ref[b] = total[b * block_rows : (b + 1) * block_rows]


def mix_sum(targets, rows):
    sources, row_count, lanes = rows.shape
    block_rows = WIDE * TGT_DEV
    return pl.pallas_call(
        mix_sum_kernel,
        out_shape=jax.ShapeDtypeStruct((STATIONS, block_rows, lanes), jnp.float32),
        grid=(STATIONS // BATCH,),
        in_specs=[
            pl.BlockSpec((1, sources * row_count), lambda i: (0, 0)),
            pl.BlockSpec(rows.shape, lambda i: (0, 0, 0)),
        ],
        out_specs=pl.BlockSpec((BATCH, block_rows, lanes), lambda i: (i, 0, 0)),
        scratch_shapes=[pltpu.VMEM((sources * row_count, 2 * lanes), jnp.bfloat16)],
        compiler_params=pltpu.CompilerParams(vmem_limit_bytes=40 << 20),
        cost_estimate=pl.CostEstimate(
            flops=4 * STATIONS * block_rows * sources * row_count * lanes,
            bytes_accessed=2 * rows.size + 4 * STATIONS * block_rows * lanes,
            transcendentals=0,
        ),
    )(targets, rows)


def ring_start(parts, station):
    def part(offset):
        return lax.dynamic_index_in_dim(parts, (station + offset) % STATIONS, 0, keepdims=False)

    return part, part(STATIONS // 2), part(STATIONS // 2 + 1)


def ring_turn(state, s):
    half = STATIONS // 2
    part, up, down = state
    up = ring_step(up, 1)
    if s < half - 1:
        up = up + part(half - 1 - s)
        down = ring_step(down, -1)
        if s < half - 2:
            down = down + part(half + 2 + s)
    return part, up, down


def exchange(values, groups):
    return lax.all_to_all(
        values, "tgt", split_axis=0, concat_axis=0, axis_index_groups=groups, tiled=True
    )


def scatter_sum(values):
    return lax.psum_scatter(
        values, "tgt", scatter_dimension=0, axis_index_groups=ring_groups, tiled=False
    )


def shards(
    exposure_flux,
    exposure_ivar,
    exposure_res,
    target_of_row,
    valid_of_row,
    rest_basis,
    redshift_shift,
):
    device = lax.axis_index("tgt")
    my_z = (device // CS) % ZS
    row_count, wave_dev = exposure_flux.shape
    masked = jnp.where(valid_of_row == 1, target_of_row, -1)
    targets = lax.dynamic_index_in_dim(
        masked.reshape(XS, ZS, CS * row_count), my_z, 1, keepdims=False
    ).reshape(1, -1)
    wide_targets = lax.dynamic_index_in_dim(
        masked.reshape(XS, STATIONS, PAIR * CS * row_count), my_z // PAIR, 1, keepdims=False
    ).reshape(1, -1)

    rows = exchange(
        split_lanes(exposure_ivar, jnp.transpose(exposure_res, (1, 0, 2))), plane_groups
    )
    band_index = lax.axis_index("band")
    shifts = lax.dynamic_slice_in_dim(redshift_shift, band_index * Z_DEV, Z_DEV)
    windows = basis_windows(rest_basis, shifts, 0, rest_basis.shape[1] - SHIFT)
    firsts, seconds = windows[:, pair_first, :], windows[:, pair_second, :]
    mixed = mix_pair(exposure_ivar, exposure_flux)
    rows, mixed, windows, firsts, seconds, wide_targets = lax.optimization_barrier(
        (rows, mixed, windows, firsts, seconds, wide_targets)
    )
    mixed = exchange(mixed, wide_groups)
    part_res = coadd_res_rows(targets, rows)
    mixed, part_res = lax.optimization_barrier((mixed, part_res))
    turns = STATIONS // 2
    part, up, down = ring_start(mix_sum(wide_targets, mixed), my_z // PAIR)
    for s in range(turns):
        part, up, down = ring_turn((part, up, down), s)
        if s < turns - 1:
            up, down = lax.optimization_barrier((up, down))
    sums = part(0) + up + down
    res_sum = scatter_sum(part_res)

    own = exchange(sums.reshape(WIDE, TGT_DEV, -1), wide_groups)
    own = jnp.transpose(own.reshape(WIDE, TGT_DEV, 2, wave_dev // WIDE), (2, 1, 0, 3))
    own = own.reshape(2, TGT_DEV, wave_dev)
    everything = lax.all_gather(own.astype(jnp.bfloat16), "band", axis=2, tiled=True)
    everything = everything.astype(jnp.float32)
    coadd_flux = own[1] / own[0]
    fit_gain = fit_from(*normal_terms(everything[0], everything[1], windows, firsts, seconds))

    back = exchange(res_sum, plane_groups)
    own_res = jnp.transpose(back, (1, 2, 0, 3)).reshape(NDIAG, TGT_DEV, wave_dev)
    coadd_res = (own_res.astype(jnp.float32) / own[0][None]).astype(jnp.bfloat16)
    return (coadd_flux, jnp.transpose(coadd_res, (1, 0, 2)), fit_gain)


def solution(mesh):
    in_specs = (P("tgt", "band"), P("tgt", "band"), P("tgt", None, "band"), P(), P(), P(), P())
    out_specs = (P("tgt", "band"), P("tgt", None, "band"), P("tgt", "band"))
    return jax.shard_map(shards, mesh=mesh, in_specs=in_specs, out_specs=out_specs, check_vma=False)
```
